32 devices in a mesh: ka: 4 (over y, x), pw: 8 (over z, core).
Axes of the slice: x: 2, y: 2, z: 4, core: 2. Of those that a mesh axis runs over, the one named last changes fastest.
Arguments:
- band_coeffs: bfloat16 [4, 2, 1024, 384], P('ka', None, 'pw'), may hold values from -6 to 6
- cutoff_weight: float32 [4, 1024], P('ka', 'pw'), may hold values from 0.3 to 3
- row_order: int32 [4, 1024], P('ka', 'pw'), may hold values from 0 to 1023, as said below
- neighbour: int32 [4], P('ka'), may hold values from 0 to 3, as said below
- gauge_matrix: bfloat16 [4, 2, 384, 384], P('ka'), may hold values from -0.21875 to 0.21875
Outputs:
- whitened: bfloat16 [4, 2, 1024, 384], P('ka', None, 'pw')
- correlations: float32 [4, 2, 2, 384, 384], P('ka')
The draws below stay inside these ranges and needn't reach their ends.
Inputs may be any that keep to these rules, and one draw needn't show every extreme that they name: `row_order`: within each aligned block of 128 entries of a row, the entries are a permutation of that block's own indices. neighbour[k] is (k + 1) mod 4 or (k - 1) mod 4; groups 0 and 1 take the second.
All inputs are finite; a program needn't handle non-finite values.
Results may differ from the reference program's by a relative error of at most 0.009.
Values may be sent and summed in bfloat16 or wider, within the bound.
A program may use at most 64 MiB of HBM per device.

```python
import math
import jax
import jax.numpy as jnp
from jax import lax

NB = 384
PW_DEV = 128
NS_STEPS = 2
NK = 4
NPW = 1024


def draw_band_coeffs(key, part):
    shape = (NK, 2, NPW, NB)
    values = jnp.clip(jax.random.normal(jax.random.fold_in(key, 41), shape, jnp.float32), -6.0, 6.0)
    return values.astype(jnp.bfloat16)


def draw_row_order(key, part):
    block_count = NK * (NPW // PW_DEV)
    subkeys = jax.random.split(jax.random.fold_in(key, 11), block_count)
    orders = jax.vmap(lambda sub_key: jax.random.permutation(sub_key, PW_DEV))(subkeys)
    offsets = jnp.arange(block_count, dtype=jnp.int32) % (NPW // PW_DEV) * PW_DEV
    return (orders.astype(jnp.int32) + offsets[:, None]).reshape(NK, NPW)


def draw_neighbour(key, part):
    signs = jax.random.randint(jax.random.fold_in(key, 23), (NK,), 0, 2).astype(jnp.int32) * 2 - 1
    positions = jnp.arange(NK, dtype=jnp.int32)
    signs = jnp.where(positions < 2, -1, signs)
    return ((positions + signs + NK) % NK).astype(jnp.int32)


def level_of(own_key, dims, pieces, least, largest):
    def one(dim, shards_of):
        heights = jax.random.uniform(jax.random.fold_in(jax.random.fold_in(own_key, 6), dim), (shards_of,), jnp.float32, least / len(pieces), largest / len(pieces))
        return jnp.repeat(jnp.exp(heights), dims[dim] // shards_of).reshape((-1,) + (1,) * (len(dims) - dim - 1))

    level = one(*pieces[0])
    for cut in pieces[1:]:
        level = level * one(*cut)
    return level


def scatter_about(own_key, shape, spread, bound, cuts=(), held_as=jnp.bfloat16):
    entries = jax.random.normal(own_key, shape, jnp.float32) * spread
    if len(cuts) > 0:
        entries = level_of(own_key, shape, cuts, -0.22, 0.18) * entries
    return jnp.clip(entries, min=-bound, max=bound).astype(held_as)


def setup_inputs(seed: int = 0) -> dict:
    streams_of = jax.random.split(jax.random.key(seed), 6)
    return {
        "band_coeffs": draw_band_coeffs(jax.random.fold_in(streams_of[5], 71), 0),
        "cutoff_weight": jnp.clip(jnp.exp(math.log(3.0) - 2.3025851 * jax.random.uniform(streams_of[1], (NK, NPW), jnp.float32) ** level_of(streams_of[1], (NK, NPW), ((0, 4), (1, 8)), -0.2, 0.2)), 0.3, 3.0),
        "row_order": draw_row_order(jax.random.fold_in(streams_of[5], 71), 0),
        "neighbour": draw_neighbour(jax.random.fold_in(streams_of[5], 71), 0),
        "gauge_matrix": scatter_about(streams_of[4], (NK, 2, NB, NB), (2 * NB) ** -0.5, 0.21875, ((0, 4),)),
    }


def precise_dot(left, right):
    return jnp.dot(left, right, precision=lax.Precision.HIGHEST, preferred_element_type=jnp.float32)

def complex_product(left_re, left_im, right_re, right_im):
    real_part = precise_dot(left_re, right_re) - precise_dot(left_im, right_im)
    imag_part = precise_dot(left_re, right_im) + precise_dot(left_im, right_re)
    return (real_part, imag_part)

def lowered_dot(left, right):
    return jnp.dot(left, right, preferred_element_type=jnp.float32)

def whitening(gram_re, gram_im, scale):
    identity = jnp.eye(gram_re.shape[0], dtype=jnp.float32)
    upper_re = gram_re / scale
    upper_im = gram_im / scale
    lower_re = identity
    lower_im = jnp.zeros_like(identity)
    for ns_turn in range(NS_STEPS):
        prod_re, prod_im = complex_product(lower_re, lower_im, upper_re, upper_im)
        middle_re = 1.5 * identity - 0.5 * prod_re
        middle_im = -0.5 * prod_im
        upper_re, upper_im = complex_product(upper_re, upper_im, middle_re, middle_im)
        lower_re, lower_im = complex_product(middle_re, middle_im, lower_re, lower_im)
    return (lower_re, lower_im)

def apply_whitening(filtered, white_re, white_im):
    wide_re = white_re.astype(jnp.bfloat16)
    wide_im = white_im.astype(jnp.bfloat16)
    out_re = lowered_dot(filtered[0], wide_re) - lowered_dot(filtered[1], wide_im)
    out_im = lowered_dot(filtered[0], wide_im) + lowered_dot(filtered[1], wide_re)
    return jnp.stack([out_re, out_im]).astype(jnp.bfloat16)

def rotate(mix_re, mix_im, own_gauge, next_gauge):
    rot_re = (lowered_dot(mix_re, next_gauge[0]) - lowered_dot(mix_im, next_gauge[1])).astype(jnp.bfloat16)
    rot_im = (lowered_dot(mix_re, next_gauge[1]) + lowered_dot(mix_im, next_gauge[0])).astype(jnp.bfloat16)
    out_re = lowered_dot(own_gauge[0].T, rot_re) + lowered_dot(own_gauge[1].T, rot_im)
    out_im = lowered_dot(own_gauge[0].T, rot_im) - lowered_dot(own_gauge[1].T, rot_re)
    return jnp.stack([out_re, out_im])

def reference(band_coeffs, cutoff_weight, row_order, neighbour, gauge_matrix):
    filtered = (band_coeffs.astype(jnp.float32) * cutoff_weight[:, None, :, None]).astype(jnp.bfloat16)

    def whiten_group(group):
        wide = group.astype(jnp.float32)
        blocks = jnp.einsum('prn,qrm->pqnm', wide, wide, precision=lax.Precision.HIGHEST)
        gram_re = blocks[0, 0] + blocks[1, 1]
        gram_im = blocks[0, 1] - blocks[1, 0]
        scale = 2.0 * jnp.sum(wide * wide) / NB
        white_re, white_im = whitening(gram_re, gram_im, scale)
        return apply_whitening(group, white_re, white_im)
    whitened = lax.map(whiten_group, filtered)
    root_scale = jnp.sqrt(jnp.float32(NPW))

    def one_direction(group_index, partner_index):
        own = whitened[group_index].astype(jnp.float32)
        other = whitened[partner_index]
        moved = jnp.take(other, row_order[group_index].astype(jnp.int32), axis=1).astype(jnp.float32)
        blocks = jnp.einsum('prn,qrm->pqnm', own, moved, precision=lax.Precision.HIGHEST)
        mix_re = ((blocks[0, 0] + blocks[1, 1]) * root_scale).astype(jnp.bfloat16)
        mix_im = ((blocks[0, 1] - blocks[1, 0]) * root_scale).astype(jnp.bfloat16)
        return rotate(mix_re, mix_im, gauge_matrix[group_index], gauge_matrix[partner_index])

    def correlation_group(group_index):
        first = neighbour[group_index].astype(jnp.int32)
        second = ((2 * group_index - first + 2 * NK) % NK).astype(jnp.int32)
        return jnp.stack([one_direction(group_index, first), one_direction(group_index, second)])
    correlations = lax.map(correlation_group, jnp.arange(NK, dtype=jnp.int32))
    return (whitened, correlations)
```

```python
import functools
import math

import jax
import jax.numpy as jnp
from jax import lax
from jax.experimental import pallas as pl
from jax.experimental.pallas import tpu as pltpu
from jax.sharding import PartitionSpec as P

MESH = pl.DeviceIdType.MESH
CORES = 2
LANES = 128
A_CHUNKS = 6
W_PIECES = 2
PARTS = 4
NEAR_STEPS = ((2, 2, 0, 0), (8, 9, 0, 2), (9, 12, 2, 6), (12, 12, 6, 8), (12, 12, 8, 10), (12, 12, 10, 12))
FAR_STEPS = ((0, 1, 0, 0), (1, 3, 0, 0), (3, 6, 0, 1), (6, 8, 1, 3), (8, 10, 3, 6), (10, 12, 6, 12))
F32 = jnp.float32
BF16 = jnp.bfloat16


def mm(left, right):
    return jnp.dot(left, right, preferred_element_type=F32)


def mm_t(left, right):
    return lax.dot_general(left, right, (((0,), (0,)), ((), ())), preferred_element_type=F32)


def complex_mm(left_re, left_im, right_re, right_im):
    width = right_re.shape[1]
    left = jnp.concatenate([left_re, left_im], axis=1)
    right = jnp.concatenate(
        [
            jnp.concatenate([right_re, right_im], axis=1),
            jnp.concatenate([-right_im, right_re], axis=1),
        ],
        axis=0,
    )
    both = mm(left, right)
    return both[:, :width], both[:, width:]


def halves(packed):
    turned = packed.T
    return 0.5 * (packed + turned), 0.5 * (packed - turned)


def kernel(
    ka_count,
    pw_count,
    bands_hbm,
    weight_hbm,
    order_hbm,
    gauge_hbm,
    neighbour_hbm,
    white_out,
    corr_out,
    bands_ref,
    weight_ref,
    order_ref,
    gauge_ref,
    neighbour_ref,
    load_sem,
    f_buf,
    p_buf,
    own_t,
    fn_buf,
    un_buf,
    a_full,
    a_local,
    a_sum,
    a_in,
    a_tot,
    a_other,
    c_local,
    c_sum,
    c_in,
    c_tot,
    w_buf,
    wn_buf,
    v_buf,
    vn_buf,
    x_buf,
    r_buf,
    pair_send,
    pair_recv,
    x_send,
    y_send,
    fn_recv,
    un_recv,
    wn_recv,
    a_send,
    a_recv,
    a_out,
    a_got,
    c_send,
    c_recv,
    c_out,
    c_got,
):
    rows, nb = bands_ref.shape[1], bands_ref.shape[2]
    loads = [
        pltpu.make_async_copy(src, dst, load_sem.at[turn])
        for turn, (src, dst) in enumerate(
            [
                (bands_hbm, bands_ref),
                (weight_hbm, weight_ref),
                (order_hbm, order_ref),
                (gauge_hbm, gauge_ref),
                (neighbour_hbm, neighbour_ref),
            ]
        )
    ]
    for load in loads:
        load.start()
    half = nb // CORES
    strips = nb // LANES
    a_rows = half // A_CHUNKS
    w_rows = half // W_PIECES
    c_total = PARTS * strips
    k = lax.axis_index("ka")
    p = lax.axis_index("pw")
    core = lax.rem(p, CORES)
    q = lax.div(p, CORES)
    line = pw_count // CORES
    ahead = lax.rem(k + 1, ka_count)
    base = q * CORES
    partner = base + 1 - core
    parity = lax.rem(k, 2)
    near = core == parity
    far = core != parity
    across = k + 1 - 2 * parity
    across_core = base + 1 - parity
    onward = lax.rem(k + 2 - 4 * parity + ka_count, ka_count)
    source = lax.rem(k - 2 + 4 * parity + ka_count, ka_count)
    edge = (q == 0) | (q == line - 1)
    inner = jnp.logical_not(edge)
    mid = (q == line // 2 - 1) | (q == line // 2)
    slot = mid.astype(jnp.int32)
    side_sign = jnp.where(2 * q < line, 1, -1)
    inward = p + CORES * side_sign
    outward = p - CORES * side_sign

    barrier = pltpu.get_barrier_semaphore()

    def greet(a, b):
        pl.semaphore_signal(barrier, inc=1, device_id=(a, b), device_id_type=MESH)

    greet(k, partner)
    greet(k, inward)

    @pl.when(near)
    def _():
        for side in range(CORES):
            greet(across, base + side)

    @pl.when(far)
    def _():
        greet(source, partner)

    @pl.when(inner)
    def _():
        greet(k, outward)

    eye = (
        lax.broadcasted_iota(jnp.int32, (nb, nb), 0) == lax.broadcasted_iota(jnp.int32, (nb, nb), 1)
    ).astype(F32)
    first = lax.broadcasted_iota(jnp.int32, (nb, nb), 0) == 0
    rest = jnp.where(first, 0.0, eye)

    for load in loads[:3]:
        load.wait()
    row_id = lax.broadcasted_iota(jnp.int32, (rows, rows), 0)
    col_id = lax.broadcasted_iota(jnp.int32, (rows, rows), 1)
    weight = jnp.sum(jnp.where(row_id == col_id, weight_ref[...], 0.0), axis=1, keepdims=True)
    pick = (row_id == order_ref[...] - p * rows).astype(BF16)
    for part in range(2):
        filtered = (bands_ref[part].astype(F32) * weight).astype(BF16)
        f_buf[part] = filtered
        p_buf[core, part] = mm(pick, filtered).astype(BF16)

    as_one = lambda flag: flag.astype(jnp.int32)
    pl.semaphore_wait(barrier, 3 + as_one(near) + as_one(inner))

    def remote(src, dst, send, recv, a, b):
        return pltpu.make_async_remote_copy(
            src_ref=src, dst_ref=dst, send_sem=send, recv_sem=recv,
            device_id=(a, b), device_id_type=MESH,
        )

    def to_pair(src, dst, turn):
        return remote(src, dst, pair_send.at[turn], pair_recv.at[turn], k, partner)

    def got_pair(dst, turn):
        remote(dst, dst, pair_send.at[turn], pair_recv.at[turn], k, partner).wait_recv()

    def to_across(src, dst, recv, turn):
        return remote(src, dst, x_send.at[turn], recv, across, across_core)

    def arrived(dst, recv):
        remote(dst, dst, x_send.at[0], recv, k, partner).wait_recv()

    def pass_on(dst, recv, turn):
        return remote(dst, dst, y_send.at[turn], recv, onward, partner)

    def strip_of(buf, t):
        return buf.at[:, :, pl.ds(t * LANES, LANES)]

    p_copy = to_pair(p_buf.at[core], p_buf.at[core], 0)
    p_copy.start()
    x_copies = [
        to_across(strip_of(f_buf, t), strip_of(fn_buf.at[core], t), fn_recv.at[core, t], t)
        for t in range(strips)
    ]
    for copy in x_copies:
        copy.start()
    for load in loads[3:]:
        load.wait()
    u_copy = to_across(gauge_ref.at[core], un_buf.at[core], un_recv.at[core], strips)
    u_copy.start()
    x_copies.append(u_copy)

    f_passed = [
        [
            pass_on(strip_of(fn_buf.at[side], t), fn_recv.at[side, t], t * CORES + side)
            for side in range(CORES)
        ]
        for t in range(strips)
    ]
    turn = strips * CORES
    u_passed = [pass_on(un_buf.at[side], un_recv.at[side], turn + side) for side in range(CORES)]
    turn += CORES
    w_parts = [(side, piece) for piece in range(W_PIECES) for side in range(CORES)]

    def w_piece(side, piece):
        return wn_buf.at[side, pl.ds(piece * w_rows, w_rows)]

    w_passed = [
        pass_on(w_piece(side, piece), wn_recv.at[side, piece], turn + n)
        for n, (side, piece) in enumerate(w_parts)
    ]

    got_pair(p_buf.at[1 - core], 0)
    own_flat = p_buf[...].reshape(CORES * 2 * rows, nb)
    turned = []
    for side in range(CORES):
        turned += [p_buf[side, 1], -p_buf[side, 0]]
    own_turned = jnp.concatenate(turned, axis=0)
    own_t[...] = own_flat.T
    gram = mm(own_t[...], own_flat) + mm(own_t[...], own_turned)
    a_full[...] = gram - (jnp.sum(gram * eye) / nb) * rest
    for i in range(A_CHUNKS):
        a_local[i] = a_full[pl.ds(pl.multiple_of(core * half + i * a_rows, 8), a_rows), :]

    def c_view(buf, i):
        t = lax.div(i, PARTS)
        part = lax.div(lax.rem(i, PARTS), 2)
        low = pl.multiple_of(lax.rem(i, 2) * half, 16)
        return buf.at[t, part, pl.ds(low, half)]

    def a_view(buf, i):
        return buf.at[i]

    def gather(view, local, total, incoming, send, recv, i):
        @pl.when(edge)
        def _():
            view(total, i)[...] = view(local, i)[...].astype(BF16)

        @pl.when(inner)
        def _():
            arrived(view(incoming.at[0], i), recv.at[0, i])
            view(total, i)[...] = (
                view(local, i)[...] + view(incoming.at[0], i)[...].astype(F32)
            ).astype(BF16)

        remote(
            view(total, i), view(incoming.at[slot], i), send.at[i], recv.at[slot, i], k, inward
        ).start()

    def spread(view, total, incoming, final, recv, out, got, i):
        @pl.when(mid)
        def _():
            arrived(view(incoming.at[1], i), recv.at[1, i])
            view(final, i)[...] = (
                view(total, i)[...].astype(F32) + view(incoming.at[1], i)[...].astype(F32)
            ).astype(BF16)

        @pl.when(jnp.logical_not(mid))
        def _():
            arrived(view(final, i), got.at[i])

        @pl.when(inner)
        def _():
            remote(view(final, i), view(final, i), out.at[i], got.at[i], k, outward).start()

    def gather_a(i):
        gather(a_view, a_local, a_sum, a_in, a_send, a_recv, i)

    def spread_a(i):
        spread(a_view, a_sum, a_in, a_tot, a_recv, a_out, a_got, i)

    def gather_c(i):
        gather(c_view, c_local, c_sum, c_in, c_send, c_recv, i)

    def spread_c(i):
        spread(c_view, c_sum, c_in, c_tot, c_recv, c_out, c_got, i)

    def over(one, start, stop):
        def step(i, carry):
            one(i)
            return carry

        lax.fori_loop(start, stop, step, 0)

    def at_cut(cut):
        return cut * c_total // 12

    def sums(turn):
        bounds = [
            jnp.where(near, at_cut(a), at_cut(b)) for a, b in zip(NEAR_STEPS[turn], FAR_STEPS[turn])
        ]
        g_low, g_high, s_low, s_high = bounds

        @pl.when(inner)
        def _():
            def one(n):
                @pl.when(g_low + n < g_high)
                def _():
                    gather_c(g_low + n)

                @pl.when(s_low + n < s_high)
                def _():
                    spread_c(s_low + n)

            over(one, 0, jnp.maximum(g_high - g_low, s_high - s_low))

    a_copy = to_pair(a_tot, a_other, 1)

    def get_strip(t, forward):
        for side in range(CORES):
            arrived(strip_of(fn_buf.at[side], t), fn_recv.at[side, t])
            if forward:
                f_passed[t][side].start()

    def cross_strip(t):
        low, high = t * LANES, (t + 1) * LANES
        plain, other = [], []
        for side in range(CORES):
            re, im = fn_buf[side, 0, :, low:high], fn_buf[side, 1, :, low:high]
            plain += [re, im]
            other += [im, -re]
        right = jnp.concatenate(
            [jnp.concatenate(plain, axis=0), jnp.concatenate(other, axis=0)], axis=1
        )
        cross = mm(own_t[...], right)
        c_local[t, 0] = cross[:, :LANES]
        c_local[t, 1] = cross[:, LANES:]

    def edge_strip(t):
        @pl.when(edge)
        def _():
            over(gather_c, PARTS * t, PARTS * (t + 1))

    @pl.when(edge)
    def _():
        over(gather_a, 0, A_CHUNKS)

    a_cuts = [A_CHUNKS * t // strips for t in range(strips + 1)]

    @pl.when(near)
    def _():
        for t in range(strips):
            get_strip(t, True)

            @pl.when(inner)
            def _():
                over(gather_a, a_cuts[t], a_cuts[t + 1])

            cross_strip(t)
            edge_strip(t)

        @pl.when(inner)
        def _():
            over(gather_c, 0, at_cut(2))
            over(spread_a, 0, A_CHUNKS // 2)
            over(gather_c, at_cut(2), at_cut(4))
            over(spread_a, A_CHUNKS // 2, A_CHUNKS)
            a_copy.start()
            over(gather_c, at_cut(4), at_cut(8))

    @pl.when(far)
    def _():
        @pl.when(inner)
        def _():
            over(gather_a, 0, A_CHUNKS)
            over(spread_a, 0, A_CHUNKS // 2)

        for t in range(strips):
            get_strip(t, False)
            cross_strip(t)
            edge_strip(t)
            if t == 0:
                @pl.when(inner)
                def _():
                    over(spread_a, A_CHUNKS // 2, A_CHUNKS)
                    a_copy.start()

    def pass_u():
        for side in range(CORES):
            arrived(un_buf.at[side], un_recv.at[side])
            u_passed[side].start()

    @pl.when(edge)
    def _():
        pl.when(near)(pass_u)
        over(spread_a, 0, A_CHUNKS)
        a_copy.start()

    sums(0)
    got_pair(a_other, 1)
    a_full[pl.ds(pl.multiple_of(core * half, 8), half), :] = (
        a_tot[...].astype(F32).reshape(half, nb)
    )
    a_full[pl.ds(pl.multiple_of((1 - core) * half, 8), half), :] = (
        a_other[...].astype(F32).reshape(half, nb)
    )

    packed = a_full[...]
    mean = jnp.sum(packed * eye)
    deviation = packed - mean * (eye - rest)
    e_re, e_im = halves(deviation / (2.0 * mean))
    e_re_b, e_im_b = e_re.astype(BF16), e_im.astype(BF16)
    sq_re, sq_im = complex_mm(e_re_b, e_im_b, e_re_b, e_im_b)
    pl.when(near & inner)(pass_u)
    sums(1)
    left_re, left_im = e_re - 0.5 * sq_re, e_im - 0.5 * sq_im
    right_re, right_im = 0.25 * sq_re - 1.25 * e_re, 0.25 * sq_im - 1.25 * e_im
    last_re, last_im = complex_mm(
        left_re.astype(BF16), left_im.astype(BF16), right_re.astype(BF16), right_im.astype(BF16)
    )
    white_re = 1.38671875 * eye - 0.75 * e_re - 0.78125 * left_re - 0.3125 * right_re - 0.5 * last_re
    white_im = -0.75 * e_im - 0.78125 * left_im - 0.3125 * right_im - 0.5 * last_im
    w_buf[...] = (white_re + white_im).astype(BF16).reshape(CORES, half, nb)
    for piece in range(W_PIECES):
        w_copy = to_across(
            w_buf.at[core, pl.ds(piece * w_rows, w_rows)], w_piece(core, piece),
            wn_recv.at[core, piece], strips + 1 + piece,
        )
        w_copy.start()
        x_copies.append(w_copy)
    w_re, w_im = white_re.astype(BF16), white_im.astype(BF16)
    sums(2)
    out_re, out_im = complex_mm(f_buf[0], f_buf[1], w_re, w_im)
    white_out[0] = out_re.astype(BF16)
    white_out[1] = out_im.astype(BF16)
    sums(3)
    root = math.sqrt(rows * pw_count)
    v_re = mm_t(gauge_ref[0], w_re) + mm_t(gauge_ref[1], w_im)
    v_im = mm_t(gauge_ref[0], w_im) - mm_t(gauge_ref[1], w_re)
    v_buf[:, :nb] = (v_re * root).astype(BF16)
    v_buf[:, nb:] = (v_im * root).astype(BF16)
    sums(4)

    @pl.when(near)
    def _():
        for n, (side, piece) in enumerate(w_parts):
            arrived(w_piece(side, piece), wn_recv.at[side, piece])
            w_passed[n].start()

    sums(5)

    @pl.when(far)
    def _():
        for side in range(CORES):
            arrived(un_buf.at[side], un_recv.at[side])
        for side, piece in w_parts:
            arrived(w_piece(side, piece), wn_recv.at[side, piece])

    next_re, next_im = halves(wn_buf[...].astype(F32).reshape(nb, nb))
    vn_re, vn_im = complex_mm(next_re.astype(BF16), next_im.astype(BF16), un_buf[0], un_buf[1])
    vn_buf[0] = vn_re.astype(BF16)
    vn_buf[1] = vn_im.astype(BF16)
    moved = None
    for t in range(strips):
        @pl.when(edge)
        def _():
            over(spread_c, PARTS * t, PARTS * (t + 1))

        low, high = t * LANES, (t + 1) * LANES
        left = jnp.concatenate([c_tot[t, 0], c_tot[t, 1]], axis=1)
        re, im = vn_buf[0, low:high], vn_buf[1, low:high]
        right = jnp.concatenate(
            [jnp.concatenate([re, im], axis=1), jnp.concatenate([-im, re], axis=1)], axis=0
        )
        if t < strips - 1:
            if t == 0:
                x_buf[...] = mm(left, right)
            else:
                x_buf[...] += mm(left, right)
        else:
            moved = x_buf[...] + mm(left, right)
    x_re, x_im = moved[:, :nb].astype(BF16), moved[:, nb:].astype(BF16)
    rights = (jnp.concatenate([x_re, -x_im], axis=0), jnp.concatenate([x_im, x_re], axis=0))
    r_copies = [to_pair(r_buf.at[core, part], r_buf.at[core, part], 2 + part) for part in range(2)]
    for part in range(2):
        r_buf[core, part] = mm(v_buf[...], rights[part]).astype(BF16)
        r_copies[part].start()

    for copy in [p_copy, a_copy] + x_copies:
        copy.wait_send()

    @pl.when(near)
    def _():
        for copy in sum(f_passed, []) + u_passed + w_passed:
            copy.wait_send()

    def settle(view, total, final, send, out, got, i):
        remote(view(total, i), view(total, i), send.at[i], got.at[i], k, partner).wait_send()

        @pl.when(inner)
        def _():
            remote(view(final, i), view(final, i), out.at[i], got.at[i], k, partner).wait_send()

    over(lambda i: settle(a_view, a_sum, a_tot, a_send, a_out, a_got, i), 0, A_CHUNKS)
    over(lambda i: settle(c_view, c_sum, c_tot, c_send, c_out, c_got, i), 0, c_total)
    for part in range(2):
        got_pair(r_buf.at[1 - core, part], 2 + part)
    looks_ahead = jnp.full((nb, nb), neighbour_ref[0], jnp.int32) == ahead
    for part in range(2):
        corr_out[0, part] = jnp.where(looks_ahead, r_buf[0, part], r_buf[1, part])
        corr_out[1, part] = jnp.where(looks_ahead, r_buf[1, part], r_buf[0, part])
    for copy in r_copies:
        copy.wait_send()


def finish(pair_hbm, white_hbm, corr_hbm, whitened_hbm, pair_ref, white_ref, corr_ref, load_sem, store_sem):
    directions = pair_ref.shape[0]
    loads = [
        pltpu.make_async_copy(pair_hbm.at[n], pair_ref.at[n], load_sem.at[n]) for n in range(directions)
    ] + [pltpu.make_async_copy(white_hbm, white_ref, load_sem.at[directions])]
    stores = [
        pltpu.make_async_copy(corr_ref.at[n], corr_hbm.at[n], store_sem.at[n]) for n in range(directions)
    ] + [pltpu.make_async_copy(white_ref, whitened_hbm, store_sem.at[directions])]
    for load in loads:
        load.start()
    for n in range(directions):
        loads[n].wait()
        corr_ref[n] = pair_ref[n].astype(F32)
        stores[n].start()
    loads[directions].wait()
    stores[directions].start()
    for store in stores:
        store.wait()


def on_device(ka_count, pw_count, band_coeffs, cutoff_weight, row_order, neighbour, gauge_matrix):
    rows, nb = band_coeffs.shape[2], band_coeffs.shape[3]
    half = nb // CORES
    strips = nb // LANES
    a_rows = half // A_CHUNKS
    c_total = PARTS * strips
    vmem = pl.BlockSpec(memory_space=pltpu.VMEM)
    hbm = pl.BlockSpec(memory_space=pltpu.HBM)
    dma = pltpu.SemaphoreType.DMA
    whitened, pair = pl.pallas_call(
        functools.partial(kernel, ka_count, pw_count),
        out_shape=(
            jax.ShapeDtypeStruct((2, rows, nb), BF16),
            jax.ShapeDtypeStruct((2, 2, nb, nb), BF16),
        ),
        in_specs=[hbm] * 5,
        out_specs=(vmem, vmem),
        scratch_shapes=[
            pltpu.VMEM((2, rows, nb), BF16),
            pltpu.VMEM((1, rows), F32),
            pltpu.VMEM((1, rows), jnp.int32),
            pltpu.VMEM((2, nb, nb), BF16),
            pltpu.SMEM((1,), jnp.int32),
            dma((5,)),
            pltpu.VMEM((2, rows, nb), BF16),
            pltpu.VMEM((CORES, 2, rows, nb), BF16),
            pltpu.VMEM((nb, CORES * 2 * rows), BF16),
            pltpu.VMEM((CORES, 2, rows, nb), BF16),
            pltpu.VMEM((2, nb, nb), BF16),
            pltpu.VMEM((nb, nb), F32),
            pltpu.VMEM((A_CHUNKS, a_rows, nb), F32),
            pltpu.VMEM((A_CHUNKS, a_rows, nb), BF16),
            pltpu.VMEM((2, A_CHUNKS, a_rows, nb), BF16),
            pltpu.VMEM((A_CHUNKS, a_rows, nb), BF16),
            pltpu.VMEM((A_CHUNKS, a_rows, nb), BF16),
            pltpu.VMEM((strips, 2, nb, LANES), F32),
            pltpu.VMEM((strips, 2, nb, LANES), BF16),
            pltpu.VMEM((2, strips, 2, nb, LANES), BF16),
            pltpu.VMEM((strips, 2, nb, LANES), BF16),
            pltpu.VMEM((CORES, half, nb), BF16),
            pltpu.VMEM((CORES, half, nb), BF16),
            pltpu.VMEM((nb, 2 * nb), BF16),
            pltpu.VMEM((2, nb, nb), BF16),
            pltpu.VMEM((nb, 2 * nb), F32),
            pltpu.VMEM((2, 2, nb, nb), BF16),
            dma((4,)),
            dma((4,)),
            dma((strips + 1 + W_PIECES,)),
            dma((CORES * (strips + 1 + W_PIECES),)),
            dma((CORES, strips)),
            dma((CORES,)),
            dma((CORES, W_PIECES)),
            dma((A_CHUNKS,)),
            dma((2, A_CHUNKS)),
            dma((A_CHUNKS,)),
            dma((A_CHUNKS,)),
            dma((c_total,)),
            dma((2, c_total)),
            dma((c_total,)),
            dma((c_total,)),
        ],
        compiler_params=pltpu.CompilerParams(
            collective_id=0, has_side_effects=True, vmem_limit_bytes=56 << 20
        ),
    )(band_coeffs[0], cutoff_weight, row_order, gauge_matrix[0], neighbour)
    correlations, whitened = pl.pallas_call(
        finish,
        out_shape=(
            jax.ShapeDtypeStruct((2, 2, nb, nb), F32),
            jax.ShapeDtypeStruct((2, rows, nb), BF16),
        ),
        in_specs=[hbm, hbm],
        out_specs=(hbm, hbm),
        scratch_shapes=[
            pltpu.VMEM((2, 2, nb, nb), BF16),
            pltpu.VMEM((2, rows, nb), BF16),
            pltpu.VMEM((2, 2, nb, nb), F32),
            dma((3,)),
            dma((3,)),
        ],
        compiler_params=pltpu.CompilerParams(vmem_limit_bytes=56 << 20),
    )(pair, whitened)
    return (whitened[None], correlations[None])


def solution(mesh):
    in_specs = (
        P("ka", None, "pw", None),
        P("ka", "pw"),
        P("ka", "pw"),
        P("ka"),
        P("ka", None, None, None),
    )
    out_specs = (P("ka", None, "pw", None), P("ka", None, None, None, None))
    return jax.shard_map(
        functools.partial(on_device, mesh.shape["ka"], mesh.shape["pw"]),
        mesh=mesh, in_specs=in_specs, out_specs=out_specs, check_vma=False,
    )
```

```python
import functools
import math

import jax
import jax.numpy as jnp
from jax import lax
from jax.experimental import pallas as pl
from jax.experimental.pallas import tpu as pltpu
from jax.sharding import PartitionSpec as P

MESH = pl.DeviceIdType.MESH
CORES = 2
LANES = 128
A_CHUNKS = 6
U_PIECES = 2
PARTS = 4
NEAR_STEPS = ((4, 8, 0, 3), (8, 12, 3, 8), (12, 12, 8, 12), (12, 12, 12, 12), (12, 12, 12, 12), (12, 12, 12, 12), (12, 12, 12, 12))
FAR_STEPS = ((0, 0, 0, 0), (0, 0, 0, 0), (0, 1, 0, 0), (1, 3, 0, 0), (3, 8, 0, 3), (8, 9, 3, 4), (9, 12, 4, 12))
F32 = jnp.float32
BF16 = jnp.bfloat16


def mm(left, right):
    return jnp.dot(left, right, preferred_element_type=F32)


def mm_t(left, right):
    return lax.dot_general(left, right, (((0,), (0,)), ((), ())), preferred_element_type=F32)


def complex_mm(left_re, left_im, right_re, right_im):
    width = right_re.shape[1]
    left = jnp.concatenate([left_re, left_im], axis=1)
    right = jnp.concatenate(
        [
            jnp.concatenate([right_re, right_im], axis=1),
            jnp.concatenate([-right_im, right_re], axis=1),
        ],
        axis=0,
    )
    both = mm(left, right)
    return both[:, :width], both[:, width:]


def halves(packed):
    turned = packed.T
    return 0.5 * (packed + turned), 0.5 * (packed - turned)


def kernel(
    ka_count,
    pw_count,
    bands_hbm,
    weight_hbm,
    order_hbm,
    gauge_hbm,
    white_out,
    corr_out,
    bands_ref,
    weight_ref,
    order_ref,
    gauge_ref,
    white_buf,
    load_sem,
    f_buf,
    p_buf,
    own_t,
    fn_buf,
    un_buf,
    a_full,
    a_local,
    a_sum,
    a_in,
    a_tot,
    a_other,
    c_local,
    c_sum,
    c_in,
    c_tot,
    an_buf,
    v_buf,
    r_buf,
    pair_send,
    pair_recv,
    x_send,
    y_send,
    fn_recv,
    un_recv,
    an_send,
    an_recv,
    a_send,
    a_recv,
    a_out,
    a_got,
    c_send,
    c_recv,
    c_out,
    c_got,
):
    rows, nb = bands_ref.shape[1], bands_ref.shape[2]
    loads = [
        pltpu.make_async_copy(src, dst, load_sem.at[turn])
        for turn, (src, dst) in enumerate(
            [
                (bands_hbm, bands_ref),
                (weight_hbm, weight_ref),
                (order_hbm, order_ref),
                (gauge_hbm, gauge_ref),
            ]
        )
    ]
    for load in loads:
        load.start()
    half = nb // CORES
    strips = nb // LANES
    a_rows = half // A_CHUNKS
    u_rows = nb // U_PIECES
    c_total = PARTS * strips
    k = lax.axis_index("ka")
    p = lax.axis_index("pw")
    core = lax.rem(p, CORES)
    q = lax.div(p, CORES)
    line = pw_count // CORES
    base = q * CORES
    partner = base + 1 - core
    parity = lax.rem(k, 2)
    near = core == parity
    far = core != parity
    across = k + 1 - 2 * parity
    across_core = base + 1 - parity
    onward = lax.rem(k + 2 - 4 * parity + ka_count, ka_count)
    source = lax.rem(k - 2 + 4 * parity + ka_count, ka_count)
    edge = (q == 0) | (q == line - 1)
    inner = jnp.logical_not(edge)
    mid = (q == line // 2 - 1) | (q == line // 2)
    slot = mid.astype(jnp.int32)
    side_sign = jnp.where(2 * q < line, 1, -1)
    inward = p + CORES * side_sign
    outward = p - CORES * side_sign

    barrier = pltpu.get_barrier_semaphore()

    def greet(a, b):
        pl.semaphore_signal(barrier, inc=1, device_id=(a, b), device_id_type=MESH)

    greet(k, partner)
    greet(k, inward)

    @pl.when(near)
    def _():
        for side in range(CORES):
            greet(across, base + side)

    @pl.when(far)
    def _():
        greet(source, partner)

    @pl.when(inner)
    def _():
        greet(k, outward)

    eye = (
        lax.broadcasted_iota(jnp.int32, (nb, nb), 0) == lax.broadcasted_iota(jnp.int32, (nb, nb), 1)
    ).astype(F32)
    first = lax.broadcasted_iota(jnp.int32, (nb, nb), 0) == 0
    rest = jnp.where(first, 0.0, eye)

    for load in loads[:3]:
        load.wait()
    row_id = lax.broadcasted_iota(jnp.int32, (rows, rows), 0)
    col_id = lax.broadcasted_iota(jnp.int32, (rows, rows), 1)
    weight = jnp.sum(jnp.where(row_id == col_id, weight_ref[...], 0.0), axis=1, keepdims=True)
    pick = (row_id == order_ref[...] - p * rows).astype(BF16)
    for part in range(2):
        filtered = (bands_ref[part].astype(F32) * weight).astype(BF16)
        f_buf[part] = filtered
        p_buf[core, part] = mm(pick, filtered).astype(BF16)

    as_one = lambda flag: flag.astype(jnp.int32)
    pl.semaphore_wait(barrier, 3 + as_one(near) + as_one(inner))

    def remote(src, dst, send, recv, a, b):
        return pltpu.make_async_remote_copy(
            src_ref=src, dst_ref=dst, send_sem=send, recv_sem=recv,
            device_id=(a, b), device_id_type=MESH,
        )

    def to_pair(src, dst, turn):
        return remote(src, dst, pair_send.at[turn], pair_recv.at[turn], k, partner)

    def got_pair(dst, turn):
        remote(dst, dst, pair_send.at[turn], pair_recv.at[turn], k, partner).wait_recv()

    def to_across(src, dst, recv, turn):
        return remote(src, dst, x_send.at[turn], recv, across, across_core)

    def arrived(dst, recv):
        remote(dst, dst, x_send.at[0], recv, k, partner).wait_recv()

    def pass_on(dst, recv, turn):
        return remote(dst, dst, y_send.at[turn], recv, onward, partner)

    def strip_of(buf, t):
        return buf.at[:, :, pl.ds(t * LANES, LANES)]

    p_copy = to_pair(p_buf.at[core], p_buf.at[core], 0)
    p_copy.start()
    x_copies = [
        to_across(strip_of(f_buf, t), strip_of(fn_buf.at[core], t), fn_recv.at[core, t], t)
        for t in range(strips)
    ]
    for copy in x_copies:
        copy.start()
    for load in loads[3:]:
        load.wait()
    u_parts = [(side, piece) for piece in range(U_PIECES) for side in range(CORES)]

    def u_piece(side, piece):
        return un_buf.at[side, pl.ds(piece * u_rows, u_rows)]

    for piece in range(U_PIECES):
        u_copy = to_across(
            gauge_ref.at[core, pl.ds(piece * u_rows, u_rows)], u_piece(core, piece),
            un_recv.at[core, piece], strips + piece,
        )
        u_copy.start()
        x_copies.append(u_copy)

    f_passed = [
        [
            pass_on(strip_of(fn_buf.at[side], t), fn_recv.at[side, t], t * CORES + side)
            for side in range(CORES)
        ]
        for t in range(strips)
    ]
    turn = strips * CORES
    u_passed = [
        pass_on(u_piece(side, piece), un_recv.at[side, piece], turn + n)
        for n, (side, piece) in enumerate(u_parts)
    ]
    turn += CORES * U_PIECES
    n_parts = [(side, i) for i in range(A_CHUNKS) for side in range(CORES)]
    n_passed = [
        pass_on(an_buf.at[side, i], an_recv.at[side, i], turn + n)
        for n, (side, i) in enumerate(n_parts)
    ]

    def pass_a():
        for n, (side, i) in enumerate(n_parts):
            arrived(an_buf.at[side, i], an_recv.at[side, i])
            n_passed[n].start()

    got_pair(p_buf.at[1 - core], 0)
    own_flat = p_buf[...].reshape(CORES * 2 * rows, nb)
    turned = []
    for side in range(CORES):
        turned += [p_buf[side, 1], -p_buf[side, 0]]
    own_turned = jnp.concatenate(turned, axis=0)
    own_t[...] = own_flat.T
    gram = mm(own_t[...], own_flat) + mm(own_t[...], own_turned)
    a_full[...] = gram - (jnp.sum(gram * eye) / nb) * rest
    for i in range(A_CHUNKS):
        a_local[i] = a_full[pl.ds(pl.multiple_of(core * half + i * a_rows, 8), a_rows), :]

    def c_view(buf, i):
        t = lax.div(i, PARTS)
        part = lax.div(lax.rem(i, PARTS), 2)
        low = pl.multiple_of(lax.rem(i, 2) * half, 16)
        return buf.at[t, part, pl.ds(low, half)]

    def a_view(buf, i):
        return buf.at[i]

    def gather(view, local, total, incoming, send, recv, i):
        @pl.when(edge)
        def _():
            view(total, i)[...] = view(local, i)[...].astype(BF16)

        @pl.when(inner)
        def _():
            arrived(view(incoming.at[0], i), recv.at[0, i])
            view(total, i)[...] = (
                view(local, i)[...] + view(incoming.at[0], i)[...].astype(F32)
            ).astype(BF16)

        remote(
            view(total, i), view(incoming.at[slot], i), send.at[i], recv.at[slot, i], k, inward
        ).start()

    def spread(view, total, incoming, final, recv, out, got, i):
        @pl.when(mid)
        def _():
            arrived(view(incoming.at[1], i), recv.at[1, i])
            view(final, i)[...] = (
                view(total, i)[...].astype(F32) + view(incoming.at[1], i)[...].astype(F32)
            ).astype(BF16)

        @pl.when(jnp.logical_not(mid))
        def _():
            arrived(view(final, i), got.at[i])

        @pl.when(inner)
        def _():
            remote(view(final, i), view(final, i), out.at[i], got.at[i], k, outward).start()

    def gather_a(i):
        gather(a_view, a_local, a_sum, a_in, a_send, a_recv, i)

    def share_a(i):
        return remote(
            a_tot.at[i], an_buf.at[core, i], an_send.at[i], an_recv.at[core, i], across, across_core
        )

    def spread_a(i):
        spread(a_view, a_sum, a_in, a_tot, a_recv, a_out, a_got, i)
        share_a(i).start()

    def gather_c(i):
        gather(c_view, c_local, c_sum, c_in, c_send, c_recv, i)

    def spread_c(i):
        spread(c_view, c_sum, c_in, c_tot, c_recv, c_out, c_got, i)

    def over(one, start, stop):
        def step(i, carry):
            one(i)
            return carry

        lax.fori_loop(start, stop, step, 0)

    def at_cut(cut):
        return cut * c_total // 12

    def sums(turn):
        bounds = [
            jnp.where(near, at_cut(a), at_cut(b)) for a, b in zip(NEAR_STEPS[turn], FAR_STEPS[turn])
        ]
        g_low, g_high, s_low, s_high = bounds

        @pl.when(inner)
        def _():
            def one(n):
                @pl.when(g_low + n < g_high)
                def _():
                    gather_c(g_low + n)

                @pl.when(s_low + n < s_high)
                def _():
                    spread_c(s_low + n)

            over(one, 0, jnp.maximum(g_high - g_low, s_high - s_low))

    a_copy = to_pair(a_tot, a_other, 1)

    def get_strip(t, forward):
        for side in range(CORES):
            arrived(strip_of(fn_buf.at[side], t), fn_recv.at[side, t])
            if forward:
                f_passed[t][side].start()

    def cross_strip(t):
        low, high = t * LANES, (t + 1) * LANES
        plain, other = [], []
        for side in range(CORES):
            re, im = fn_buf[side, 0, :, low:high], fn_buf[side, 1, :, low:high]
            plain += [re, im]
            other += [im, -re]
        right = jnp.concatenate(
            [jnp.concatenate(plain, axis=0), jnp.concatenate(other, axis=0)], axis=1
        )
        cross = mm(own_t[...], right)
        c_local[t, 0] = cross[:, :LANES]
        c_local[t, 1] = cross[:, LANES:]

    def edge_strip(t):
        @pl.when(edge)
        def _():
            over(gather_c, PARTS * t, PARTS * (t + 1))

    def pass_u(piece):
        for n, (side, own) in enumerate(u_parts):
            if own == piece:
                arrived(u_piece(side, piece), un_recv.at[side, piece])
                u_passed[n].start()

    @pl.when(edge)
    def _():
        over(gather_a, 0, A_CHUNKS)

    a_cuts = [A_CHUNKS * t // strips for t in range(strips + 1)]

    @pl.when(near)
    def _():
        for t in range(strips):
            get_strip(t, True)

            @pl.when(inner)
            def _():
                over(gather_a, a_cuts[t], a_cuts[t + 1])

            cross_strip(t)
            edge_strip(t)

        @pl.when(inner)
        def _():
            over(gather_c, 0, at_cut(2))
            over(spread_a, 0, A_CHUNKS // 2)
            over(gather_c, at_cut(2), at_cut(4))
            over(spread_a, A_CHUNKS // 2, A_CHUNKS)
            a_copy.start()
            pass_u(0)
            sums(0)

    @pl.when(far)
    def _():
        @pl.when(inner)
        def _():
            over(gather_a, 0, A_CHUNKS)
            over(spread_a, 0, A_CHUNKS)
            a_copy.start()

        for t in range(strips):
            get_strip(t, False)
            cross_strip(t)
            edge_strip(t)

    @pl.when(edge)
    def _():
        @pl.when(near)
        def _():
            for piece in range(U_PIECES):
                pass_u(piece)

        over(spread_a, 0, A_CHUNKS)
        a_copy.start()
        pl.when(near)(pass_a)

    @pl.when(near & inner)
    def _():
        for piece in range(1, U_PIECES):
            pass_u(piece)

    sums(1)
    pl.when(near & inner)(pass_a)
    sums(2)
    got_pair(a_other, 1)
    a_full[pl.ds(pl.multiple_of(core * half, 8), half), :] = (
        a_tot[...].astype(F32).reshape(half, nb)
    )
    a_full[pl.ds(pl.multiple_of((1 - core) * half, 8), half), :] = (
        a_other[...].astype(F32).reshape(half, nb)
    )

    def newton(packed, between):
        mean = jnp.sum(packed * eye)
        deviation = packed - mean * (eye - rest)
        e_re, e_im = halves(deviation * (0.5 / mean))
        e_re_b, e_im_b = e_re.astype(BF16), e_im.astype(BF16)
        sq_re, sq_im = complex_mm(e_re_b, e_im_b, e_re_b, e_im_b)
        between()
        left_re, left_im = e_re - 0.5 * sq_re, e_im - 0.5 * sq_im
        right_re, right_im = 0.25 * sq_re - 1.25 * e_re, 0.25 * sq_im - 1.25 * e_im
        last_re, last_im = complex_mm(
            left_re.astype(BF16), left_im.astype(BF16), right_re.astype(BF16), right_im.astype(BF16)
        )
        white_re = (
            1.38671875 * eye - 0.75 * e_re - 0.78125 * left_re - 0.3125 * right_re - 0.5 * last_re
        )
        white_im = -0.75 * e_im - 0.78125 * left_im - 0.3125 * right_im - 0.5 * last_im
        return white_re.astype(BF16), white_im.astype(BF16)

    w_re, w_im = newton(a_full[...], lambda: sums(3))
    sums(4)
    out_re, out_im = complex_mm(f_buf[0], f_buf[1], w_re, w_im)
    white_buf[0] = out_re.astype(BF16)
    white_buf[1] = out_im.astype(BF16)
    stores = [pltpu.make_async_copy(white_buf, white_out, load_sem.at[4])]
    stores[0].start()
    sums(5)
    root = math.sqrt(rows * pw_count)
    v_re = mm_t(gauge_ref[0], w_re) + mm_t(gauge_ref[1], w_im)
    v_im = mm_t(gauge_ref[0], w_im) - mm_t(gauge_ref[1], w_re)
    v_buf[:, :nb] = (v_re * root).astype(BF16)
    v_buf[:, nb:] = (v_im * root).astype(BF16)
    sums(6)

    @pl.when(far)
    def _():
        for side, piece in u_parts:
            arrived(u_piece(side, piece), un_recv.at[side, piece])
        for side, i in n_parts:
            arrived(an_buf.at[side, i], an_recv.at[side, i])

    next_re, next_im = newton(an_buf[...].astype(F32).reshape(nb, nb), lambda: None)
    vn_re, vn_im = complex_mm(next_re, next_im, un_buf[0], un_buf[1])
    vn_re, vn_im = vn_re.astype(BF16), vn_im.astype(BF16)
    moved = None
    for low, high in ((0, strips - 1), (strips - 1, strips)):
        @pl.when(edge)
        def _():
            over(spread_c, PARTS * low, PARTS * high)

        left = jnp.concatenate(
            [c_tot[t, part] for part in range(2) for t in range(low, high)], axis=1
        )
        re, im = vn_re[low * LANES : high * LANES], vn_im[low * LANES : high * LANES]
        right = jnp.concatenate(
            [jnp.concatenate([re, im], axis=1), jnp.concatenate([-im, re], axis=1)], axis=0
        )
        moved = mm(left, right) if low == 0 else moved + mm(left, right)
    x_re, x_im = moved[:, :nb].astype(BF16), moved[:, nb:].astype(BF16)
    right = jnp.concatenate(
        [jnp.concatenate([x_re, x_im], axis=1), jnp.concatenate([-x_im, x_re], axis=1)], axis=0
    )
    blocks = [(0, 0, nb), (1, 0, nb - 2 * LANES), (1, nb - 2 * LANES, nb)]
    r_copies = []
    for n, (part, low, high) in enumerate(blocks):
        cols = pl.ds(low, high - low)
        own, there = r_buf.at[part, :, cols], corr_out.at[core, part, :, cols]
        r_copies.append(to_pair(own, there, 2 + n))
        stores.append(pltpu.make_async_copy(own, there, load_sem.at[5 + n]))
    edge_col = 2 * nb - 2 * LANES
    result = mm(v_buf[...], right[:, :edge_col])
    r_buf[0] = result[:, :nb].astype(BF16)
    r_copies[0].start()
    stores[1].start()
    r_buf[1, :, : nb - 2 * LANES] = result[:, nb:].astype(BF16)
    r_copies[1].start()
    stores[2].start()
    r_buf[1, :, nb - 2 * LANES :] = mm(v_buf[...], right[:, edge_col:]).astype(BF16)
    r_copies[2].start()
    stores[3].start()

    for copy in [p_copy, a_copy] + x_copies:
        copy.wait_send()

    @pl.when(near)
    def _():
        for copy in sum(f_passed, []) + u_passed + n_passed:
            copy.wait_send()

    def settle(view, total, final, send, out, got, i):
        remote(view(total, i), view(total, i), send.at[i], got.at[i], k, partner).wait_send()

        @pl.when(inner)
        def _():
            remote(view(final, i), view(final, i), out.at[i], got.at[i], k, partner).wait_send()

    over(lambda i: share_a(i).wait_send(), 0, A_CHUNKS)
    over(lambda i: settle(a_view, a_sum, a_tot, a_send, a_out, a_got, i), 0, A_CHUNKS)
    over(lambda i: settle(c_view, c_sum, c_tot, c_send, c_out, c_got, i), 0, c_total)
    for n, (part, low, high) in enumerate(blocks):
        got_pair(corr_out.at[1 - core, part, :, pl.ds(low, high - low)], 2 + n)
    for store in stores:
        store.wait()
    for copy in r_copies:
        copy.wait_send()


def finish(
    ka_count, pair_hbm, white_hbm, neighbour_hbm, corr_hbm, whitened_hbm,
    pair_ref, white_ref, neighbour_ref, corr_ref, load_sem, store_sem,
):
    parts = [(d, part) for d in range(2) for part in range(2)]
    order = pltpu.make_async_copy(neighbour_hbm, neighbour_ref, load_sem.at[5])
    order.start()
    loads = [
        pltpu.make_async_copy(pair_hbm.at[d, part], pair_ref.at[d, part], load_sem.at[n])
        for n, (d, part) in enumerate(parts)
    ] + [pltpu.make_async_copy(white_hbm, white_ref, load_sem.at[4])]
    for load in loads:
        load.start()
    order.wait()
    looks_ahead = neighbour_ref[0] == lax.rem(lax.axis_index("ka") + 1, ka_count)
    flip = 1 - looks_ahead.astype(jnp.int32)
    stores = [
        pltpu.make_async_copy(
            corr_ref.at[d, part], corr_hbm.at[d + flip - 2 * d * flip, part], store_sem.at[n]
        )
        for n, (d, part) in enumerate(parts)
    ] + [pltpu.make_async_copy(white_ref, whitened_hbm, store_sem.at[4])]
    for n, (d, part) in enumerate(parts):
        loads[n].wait()
        corr_ref[d, part] = pair_ref[d, part].astype(F32)
        stores[n].start()
    loads[4].wait()
    stores[4].start()
    for store in stores:
        store.wait()


def on_device(ka_count, pw_count, band_coeffs, cutoff_weight, row_order, neighbour, gauge_matrix):
    rows, nb = band_coeffs.shape[2], band_coeffs.shape[3]
    half = nb // CORES
    strips = nb // LANES
    a_rows = half // A_CHUNKS
    c_total = PARTS * strips
    hbm = pl.BlockSpec(memory_space=pltpu.HBM)
    dma = pltpu.SemaphoreType.DMA
    whitened, pair = pl.pallas_call(
        functools.partial(kernel, ka_count, pw_count),
        out_shape=(
            jax.ShapeDtypeStruct((2, rows, nb), BF16),
            jax.ShapeDtypeStruct((2, 2, nb, nb), BF16),
        ),
        in_specs=[hbm] * 4,
        out_specs=(hbm, hbm),
        scratch_shapes=[
            pltpu.VMEM((2, rows, nb), BF16),
            pltpu.VMEM((1, rows), F32),
            pltpu.VMEM((1, rows), jnp.int32),
            pltpu.VMEM((2, nb, nb), BF16),
            pltpu.VMEM((2, rows, nb), BF16),
            dma((8,)),
            pltpu.VMEM((2, rows, nb), BF16),
            pltpu.VMEM((CORES, 2, rows, nb), BF16),
            pltpu.VMEM((nb, CORES * 2 * rows), BF16),
            pltpu.VMEM((CORES, 2, rows, nb), BF16),
            pltpu.VMEM((2, nb, nb), BF16),
            pltpu.VMEM((nb, nb), F32),
            pltpu.VMEM((A_CHUNKS, a_rows, nb), F32),
            pltpu.VMEM((A_CHUNKS, a_rows, nb), BF16),
            pltpu.VMEM((2, A_CHUNKS, a_rows, nb), BF16),
            pltpu.VMEM((A_CHUNKS, a_rows, nb), BF16),
            pltpu.VMEM((A_CHUNKS, a_rows, nb), BF16),
            pltpu.VMEM((strips, 2, nb, LANES), F32),
            pltpu.VMEM((strips, 2, nb, LANES), BF16),
            pltpu.VMEM((2, strips, 2, nb, LANES), BF16),
            pltpu.VMEM((strips, 2, nb, LANES), BF16),
            pltpu.VMEM((CORES, A_CHUNKS, a_rows, nb), BF16),
            pltpu.VMEM((nb, 2 * nb), BF16),
            pltpu.VMEM((2, nb, nb), BF16),
            dma((5,)),
            dma((5,)),
            dma((strips + U_PIECES,)),
            dma((CORES * (strips + U_PIECES + A_CHUNKS),)),
            dma((CORES, strips)),
            dma((CORES, U_PIECES)),
            dma((A_CHUNKS,)),
            dma((CORES, A_CHUNKS)),
            dma((A_CHUNKS,)),
            dma((2, A_CHUNKS)),
            dma((A_CHUNKS,)),
            dma((A_CHUNKS,)),
            dma((c_total,)),
            dma((2, c_total)),
            dma((c_total,)),
            dma((c_total,)),
        ],
        compiler_params=pltpu.CompilerParams(
            collective_id=0, has_side_effects=True, vmem_limit_bytes=56 << 20
        ),
    )(band_coeffs[0], cutoff_weight, row_order, gauge_matrix[0])
    correlations, whitened = pl.pallas_call(
        functools.partial(finish, ka_count),
        out_shape=(
            jax.ShapeDtypeStruct((2, 2, nb, nb), F32),
            jax.ShapeDtypeStruct((2, rows, nb), BF16),
        ),
        in_specs=[hbm, hbm, hbm],
        out_specs=(hbm, hbm),
        scratch_shapes=[
            pltpu.VMEM((2, 2, nb, nb), BF16),
            pltpu.VMEM((2, rows, nb), BF16),
            pltpu.SMEM((1,), jnp.int32),
            pltpu.VMEM((2, 2, nb, nb), F32),
            dma((6,)),
            dma((5,)),
        ],
        compiler_params=pltpu.CompilerParams(vmem_limit_bytes=56 << 20),
    )(pair, whitened, neighbour)
    return (whitened[None], correlations[None])


def solution(mesh):
    in_specs = (
        P("ka", None, "pw", None),
        P("ka", "pw"),
        P("ka", "pw"),
        P("ka"),
        P("ka", None, None, None),
    )
    out_specs = (P("ka", None, "pw", None), P("ka", None, None, None, None))
    return jax.shard_map(
        functools.partial(on_device, mesh.shape["ka"], mesh.shape["pw"]),
        mesh=mesh, in_specs=in_specs, out_specs=out_specs, check_vma=False,
    )
```

```python
import functools
import math

import jax
import jax.numpy as jnp
from jax import lax
from jax.experimental import pallas as pl
from jax.experimental.pallas import tpu as pltpu
from jax.sharding import PartitionSpec as P

MESH = pl.DeviceIdType.MESH
CORES = 2
LANES = 128
A_CHUNKS = 6
U_PIECES = 2
PARTS = 4
NEAR_STEPS = ((4, 8, 0, 3), (8, 12, 3, 8), (12, 12, 8, 12), (12, 12, 12, 12), (12, 12, 12, 12), (12, 12, 12, 12), (12, 12, 12, 12))
FAR_STEPS = ((0,0,0,0),(0,0,0,0),(0,1,0,0),(1,3,0,0),(3,9,0,3),(9,12,3,6),(12,12,6,12))
F32 = jnp.float32
BF16 = jnp.bfloat16


def mm(left, right):
    return jnp.dot(left, right, preferred_element_type=F32)


def mm_t(left, right):
    return lax.dot_general(left, right, (((0,), (0,)), ((), ())), preferred_element_type=F32)


def complex_mm(left_re, left_im, right_re, right_im):
    width = right_re.shape[1]
    left = jnp.concatenate([left_re, left_im], axis=1)
    right = jnp.concatenate(
        [
            jnp.concatenate([right_re, right_im], axis=1),
            jnp.concatenate([-right_im, right_re], axis=1),
        ],
        axis=0,
    )
    both = mm(left, right)
    return both[:, :width], both[:, width:]


def halves(packed):
    turned = packed.T
    return 0.5 * (packed + turned), 0.5 * (packed - turned)


def kernel(
    ka_count,
    pw_count,
    bands_hbm,
    weight_hbm,
    order_hbm,
    gauge_hbm,
    white_out,
    corr_out,
    bands_ref,
    weight_ref,
    order_ref,
    gauge_ref,
    white_buf,
    load_sem,
    f_buf,
    p_buf,
    own_t,
    fn_buf,
    un_buf,
    a_full,
    a_local,
    a_sum,
    a_in,
    a_tot,
    a_other,
    c_local,
    c_sum,
    c_in,
    c_tot,
    an_buf,
    v_buf,
    x_buf,
    r_buf,
    pair_send,
    pair_recv,
    x_send,
    y_send,
    fn_recv,
    un_recv,
    an_send,
    an_recv,
    a_send,
    a_recv,
    a_out,
    a_got,
    c_send,
    c_recv,
    c_out,
    c_got,
):
    rows, nb = bands_ref.shape[1], bands_ref.shape[2]
    loads = [
        pltpu.make_async_copy(src, dst, load_sem.at[turn])
        for turn, (src, dst) in enumerate(
            [
                (bands_hbm, bands_ref),
                (weight_hbm, weight_ref),
                (order_hbm, order_ref),
                (gauge_hbm, gauge_ref),
            ]
        )
    ]
    for load in loads:
        load.start()
    half = nb // CORES
    strips = nb // LANES
    a_rows = half // A_CHUNKS
    u_rows = nb // U_PIECES
    c_total = PARTS * strips
    k = lax.axis_index("ka")
    p = lax.axis_index("pw")
    core = lax.rem(p, CORES)
    q = lax.div(p, CORES)
    line = pw_count // CORES
    base = q * CORES
    partner = base + 1 - core
    parity = lax.rem(k, 2)
    near = core == parity
    far = core != parity
    across = k + 1 - 2 * parity
    across_core = base + 1 - parity
    onward = lax.rem(k + 2 - 4 * parity + ka_count, ka_count)
    source = lax.rem(k - 2 + 4 * parity + ka_count, ka_count)
    edge = (q == 0) | (q == line - 1)
    inner = jnp.logical_not(edge)
    mid = (q == line // 2 - 1) | (q == line // 2)
    slot = mid.astype(jnp.int32)
    side_sign = jnp.where(2 * q < line, 1, -1)
    inward = p + CORES * side_sign
    outward = p - CORES * side_sign

    barrier = pltpu.get_barrier_semaphore()

    def greet(a, b):
        pl.semaphore_signal(barrier, inc=1, device_id=(a, b), device_id_type=MESH)

    greet(k, partner)
    greet(k, inward)

    @pl.when(near)
    def _():
        for side in range(CORES):
            greet(across, base + side)

    @pl.when(far)
    def _():
        greet(source, partner)

    @pl.when(inner)
    def _():
        greet(k, outward)

    eye = (
        lax.broadcasted_iota(jnp.int32, (nb, nb), 0) == lax.broadcasted_iota(jnp.int32, (nb, nb), 1)
    ).astype(F32)
    first = lax.broadcasted_iota(jnp.int32, (nb, nb), 0) == 0
    rest = jnp.where(first, 0.0, eye)

    for load in loads[:3]:
        load.wait()
    row_id = lax.broadcasted_iota(jnp.int32, (rows, rows), 0)
    col_id = lax.broadcasted_iota(jnp.int32, (rows, rows), 1)
    weight = jnp.sum(jnp.where(row_id == col_id, weight_ref[...], 0.0), axis=1, keepdims=True)
    pick = (row_id == order_ref[...] - p * rows).astype(BF16)
    for part in range(2):
        filtered = (bands_ref[part].astype(F32) * weight).astype(BF16)
        f_buf[part] = filtered
        p_buf[core, part] = mm(pick, filtered).astype(BF16)

    as_one = lambda flag: flag.astype(jnp.int32)
    pl.semaphore_wait(barrier, 3 + as_one(near) + as_one(inner))

    def remote(src, dst, send, recv, a, b):
        return pltpu.make_async_remote_copy(
            src_ref=src, dst_ref=dst, send_sem=send, recv_sem=recv,
            device_id=(a, b), device_id_type=MESH,
        )

    def to_pair(src, dst, turn):
        return remote(src, dst, pair_send.at[turn], pair_recv.at[turn], k, partner)

    def got_pair(dst, turn):
        remote(dst, dst, pair_send.at[turn], pair_recv.at[turn], k, partner).wait_recv()

    def to_across(src, dst, recv, turn):
        return remote(src, dst, x_send.at[turn], recv, across, across_core)

    def arrived(dst, recv):
        remote(dst, dst, x_send.at[0], recv, k, partner).wait_recv()

    def pass_on(dst, recv, turn):
        return remote(dst, dst, y_send.at[turn], recv, onward, partner)

    def strip_of(buf, t):
        return buf.at[:, :, pl.ds(t * LANES, LANES)]

    p_copy = to_pair(p_buf.at[core], p_buf.at[core], 0)
    p_copy.start()
    x_copies = [
        to_across(strip_of(f_buf, t), strip_of(fn_buf.at[core], t), fn_recv.at[core, t], t)
        for t in range(strips)
    ]
    for copy in x_copies:
        copy.start()
    for load in loads[3:]:
        load.wait()
    u_parts = [(side, piece) for piece in range(U_PIECES) for side in range(CORES)]

    def u_piece(side, piece):
        return un_buf.at[side, pl.ds(piece * u_rows, u_rows)]

    for piece in range(U_PIECES):
        u_copy = to_across(
            gauge_ref.at[core, pl.ds(piece * u_rows, u_rows)], u_piece(core, piece),
            un_recv.at[core, piece], strips + piece,
        )
        u_copy.start()
        x_copies.append(u_copy)

    f_passed = [
        [
            pass_on(strip_of(fn_buf.at[side], t), fn_recv.at[side, t], t * CORES + side)
            for side in range(CORES)
        ]
        for t in range(strips)
    ]
    turn = strips * CORES
    u_passed = [
        pass_on(u_piece(side, piece), un_recv.at[side, piece], turn + n)
        for n, (side, piece) in enumerate(u_parts)
    ]
    turn += CORES * U_PIECES
    n_parts = [(side, i) for i in range(A_CHUNKS) for side in range(CORES)]
    n_passed = [
        pass_on(an_buf.at[side, i], an_recv.at[side, i], turn + n)
        for n, (side, i) in enumerate(n_parts)
    ]

    def pass_a():
        for n, (side, i) in enumerate(n_parts):
            arrived(an_buf.at[side, i], an_recv.at[side, i])
            n_passed[n].start()

    got_pair(p_buf.at[1 - core], 0)
    own_flat = p_buf[...].reshape(CORES * 2 * rows, nb)
    turned = []
    for side in range(CORES):
        turned += [p_buf[side, 1], -p_buf[side, 0]]
    own_turned = jnp.concatenate(turned, axis=0)
    own_t[...] = own_flat.T
    gram = mm(own_t[...], own_flat) + mm(own_t[...], own_turned)
    a_full[...] = gram - (jnp.sum(gram * eye) / nb) * rest
    for i in range(A_CHUNKS):
        a_local[i] = a_full[pl.ds(pl.multiple_of(core * half + i * a_rows, 8), a_rows), :]

    def c_view(buf, i):
        t = lax.div(i, PARTS)
        part = lax.div(lax.rem(i, PARTS), 2)
        low = pl.multiple_of(lax.rem(i, 2) * half, 16)
        return buf.at[t, part, pl.ds(low, half)]

    def a_view(buf, i):
        return buf.at[i]

    def gather(view, local, total, incoming, send, recv, i):
        @pl.when(edge)
        def _():
            view(total, i)[...] = view(local, i)[...].astype(BF16)

        @pl.when(inner)
        def _():
            arrived(view(incoming.at[0], i), recv.at[0, i])
            view(total, i)[...] = (
                view(local, i)[...] + view(incoming.at[0], i)[...].astype(F32)
            ).astype(BF16)

        remote(
            view(total, i), view(incoming.at[slot], i), send.at[i], recv.at[slot, i], k, inward
        ).start()

    def spread(view, total, incoming, final, recv, out, got, i):
        @pl.when(mid)
        def _():
            arrived(view(incoming.at[1], i), recv.at[1, i])
            view(final, i)[...] = (
                view(total, i)[...].astype(F32) + view(incoming.at[1], i)[...].astype(F32)
            ).astype(BF16)

        @pl.when(jnp.logical_not(mid))
        def _():
            arrived(view(final, i), got.at[i])

        @pl.when(inner)
        def _():
            remote(view(final, i), view(final, i), out.at[i], got.at[i], k, outward).start()

    def gather_a(i):
        gather(a_view, a_local, a_sum, a_in, a_send, a_recv, i)

    def share_a(i):
        return remote(
            a_tot.at[i], an_buf.at[core, i], an_send.at[i], an_recv.at[core, i], across, across_core
        )

    def spread_a(i):
        spread(a_view, a_sum, a_in, a_tot, a_recv, a_out, a_got, i)
        share_a(i).start()

    def gather_c(i):
        gather(c_view, c_local, c_sum, c_in, c_send, c_recv, i)

    def spread_c(i):
        spread(c_view, c_sum, c_in, c_tot, c_recv, c_out, c_got, i)

    def over(one, start, stop):
        def step(i, carry):
            one(i)
            return carry

        lax.fori_loop(start, stop, step, 0)

    def at_cut(cut):
        return cut * c_total // 12

    def sums(turn):
        bounds = [
            jnp.where(near, at_cut(a), at_cut(b)) for a, b in zip(NEAR_STEPS[turn], FAR_STEPS[turn])
        ]
        g_low, g_high, s_low, s_high = bounds

        @pl.when(inner)
        def _():
            def one(n):
                @pl.when(g_low + n < g_high)
                def _():
                    gather_c(g_low + n)

                @pl.when(s_low + n < s_high)
                def _():
                    spread_c(s_low + n)

            over(one, 0, jnp.maximum(g_high - g_low, s_high - s_low))

    a_copy = to_pair(a_tot, a_other, 1)

    def get_strip(t, forward):
        for side in range(CORES):
            arrived(strip_of(fn_buf.at[side], t), fn_recv.at[side, t])
            if forward:
                f_passed[t][side].start()

    def cross_strip(t):
        low, high = t * LANES, (t + 1) * LANES
        plain, other = [], []
        for side in range(CORES):
            re, im = fn_buf[side, 0, :, low:high], fn_buf[side, 1, :, low:high]
            plain += [re, im]
            other += [im, -re]
        right = jnp.concatenate(
            [jnp.concatenate(plain, axis=0), jnp.concatenate(other, axis=0)], axis=1
        )
        cross = mm(own_t[...], right)
        c_local[t, 0] = cross[:, :LANES]
        c_local[t, 1] = cross[:, LANES:]

    def edge_strip(t):
        @pl.when(edge)
        def _():
            over(gather_c, PARTS * t, PARTS * (t + 1))

    def pass_u(piece):
        for n, (side, own) in enumerate(u_parts):
            if own == piece:
                arrived(u_piece(side, piece), un_recv.at[side, piece])
                u_passed[n].start()

    @pl.when(edge)
    def _():
        over(gather_a, 0, A_CHUNKS)

    a_cuts = [A_CHUNKS * t // strips for t in range(strips + 1)]

    @pl.when(near)
    def _():
        for t in range(strips):
            get_strip(t, True)

            @pl.when(inner)
            def _():
                over(gather_a, a_cuts[t], a_cuts[t + 1])

            cross_strip(t)
            edge_strip(t)

        @pl.when(inner)
        def _():
            over(gather_c, 0, at_cut(2))
            over(spread_a, 0, A_CHUNKS // 2)
            over(gather_c, at_cut(2), at_cut(4))
            over(spread_a, A_CHUNKS // 2, A_CHUNKS)
            a_copy.start()
            pass_u(0)
            sums(0)

    @pl.when(far)
    def _():
        @pl.when(inner)
        def _():
            over(gather_a, 0, A_CHUNKS)
            over(spread_a, 0, A_CHUNKS)
            a_copy.start()

        for t in range(strips):
            get_strip(t, False)
            cross_strip(t)
            edge_strip(t)

    @pl.when(edge)
    def _():
        @pl.when(near)
        def _():
            for piece in range(U_PIECES):
                pass_u(piece)

        over(spread_a, 0, A_CHUNKS)
        a_copy.start()
        pl.when(near)(pass_a)

    @pl.when(near & inner)
    def _():
        for piece in range(1, U_PIECES):
            pass_u(piece)

    sums(1)
    pl.when(near & inner)(pass_a)
    sums(2)
    got_pair(a_other, 1)
    a_full[pl.ds(pl.multiple_of(core * half, 8), half), :] = (
        a_tot[...].astype(F32).reshape(half, nb)
    )
    a_full[pl.ds(pl.multiple_of((1 - core) * half, 8), half), :] = (
        a_other[...].astype(F32).reshape(half, nb)
    )

    def newton(packed, between):
        mean = jnp.sum(packed * eye)
        deviation = packed - mean * (eye - rest)
        e_re, e_im = halves(deviation * (0.5 / mean))
        e_re_b, e_im_b = e_re.astype(BF16), e_im.astype(BF16)
        sq_re, sq_im = complex_mm(e_re_b, e_im_b, e_re_b, e_im_b)
        between()
        left_re, left_im = e_re - 0.5 * sq_re, e_im - 0.5 * sq_im
        right_re, right_im = 0.25 * sq_re - 1.25 * e_re, 0.25 * sq_im - 1.25 * e_im
        last_re, last_im = complex_mm(
            left_re.astype(BF16), left_im.astype(BF16), right_re.astype(BF16), right_im.astype(BF16)
        )
        white_re = (
            1.38671875 * eye - 0.75 * e_re - 0.78125 * left_re - 0.3125 * right_re - 0.5 * last_re
        )
        white_im = -0.75 * e_im - 0.78125 * left_im - 0.3125 * right_im - 0.5 * last_im
        return white_re.astype(BF16), white_im.astype(BF16)

    w_re, w_im = newton(a_full[...], lambda: sums(3))
    sums(4)
    out_re, out_im = complex_mm(f_buf[0], f_buf[1], w_re, w_im)
    white_buf[0] = out_re.astype(BF16)
    white_buf[1] = out_im.astype(BF16)
    stores = [pltpu.make_async_copy(white_buf, white_out, load_sem.at[4])]
    stores[0].start()
    sums(5)
    root = math.sqrt(rows * pw_count)
    v_re = mm_t(gauge_ref[0], w_re) + mm_t(gauge_ref[1], w_im)
    v_im = mm_t(gauge_ref[0], w_im) - mm_t(gauge_ref[1], w_re)
    v_buf[:, :nb] = (v_re * root).astype(BF16)
    v_buf[:, nb:] = (v_im * root).astype(BF16)
    sums(6)

    @pl.when(far)
    def _():
        for side, piece in u_parts:
            arrived(u_piece(side, piece), un_recv.at[side, piece])
        for side, i in n_parts:
            arrived(an_buf.at[side, i], an_recv.at[side, i])

    next_re, next_im = newton(an_buf[...].astype(F32).reshape(nb, nb), lambda: None)
    vn_re, vn_im = complex_mm(next_re, next_im, un_buf[0], un_buf[1])
    vn_re, vn_im = vn_re.astype(BF16), vn_im.astype(BF16)
    moved = None
    for low, high in ((0, strips - 1), (strips - 1, strips)):
        @pl.when(edge)
        def _():
            over(spread_c, PARTS * low, PARTS * high)

        left = jnp.concatenate(
            [c_tot[t, part] for part in range(2) for t in range(low, high)], axis=1
        )
        re, im = vn_re[low * LANES : high * LANES], vn_im[low * LANES : high * LANES]
        right = jnp.concatenate(
            [jnp.concatenate([re, im], axis=1), jnp.concatenate([-im, re], axis=1)], axis=0
        )
        if low == 0:
            x_buf[...] = mm(left, right)
        else:
            moved = x_buf[...] + mm(left, right)
    x_re, x_im = moved[:, :nb].astype(BF16), moved[:, nb:].astype(BF16)
    right = jnp.concatenate(
        [jnp.concatenate([x_re, x_im], axis=1), jnp.concatenate([-x_im, x_re], axis=1)], axis=0
    )
    blocks = [(0, 0, nb), (1, 0, nb - 2 * LANES), (1, nb - 2 * LANES, nb)]
    r_copies = []
    for n, (part, low, high) in enumerate(blocks):
        cols = pl.ds(low, high - low)
        own, there = r_buf.at[part, :, cols], corr_out.at[core, part, :, cols]
        r_copies.append(to_pair(own, there, 2 + n))
        stores.append(pltpu.make_async_copy(own, there, load_sem.at[5 + n]))
    edge_col = 2 * nb - 2 * LANES
    result = mm(v_buf[...], right[:, :edge_col])
    r_buf[0] = result[:, :nb].astype(BF16)
    r_copies[0].start()
    stores[1].start()
    r_buf[1, :, : nb - 2 * LANES] = result[:, nb:].astype(BF16)
    r_copies[1].start()
    stores[2].start()
    r_buf[1, :, nb - 2 * LANES :] = mm(v_buf[...], right[:, edge_col:]).astype(BF16)
    r_copies[2].start()
    stores[3].start()

    for copy in [p_copy, a_copy] + x_copies:
        copy.wait_send()

    @pl.when(near)
    def _():
        for copy in sum(f_passed, []) + u_passed + n_passed:
            copy.wait_send()

    def settle(view, total, final, send, out, got, i):
        remote(view(total, i), view(total, i), send.at[i], got.at[i], k, partner).wait_send()

        @pl.when(inner)
        def _():
            remote(view(final, i), view(final, i), out.at[i], got.at[i], k, partner).wait_send()

    over(lambda i: share_a(i).wait_send(), 0, A_CHUNKS)
    over(lambda i: settle(a_view, a_sum, a_tot, a_send, a_out, a_got, i), 0, A_CHUNKS)
    over(lambda i: settle(c_view, c_sum, c_tot, c_send, c_out, c_got, i), 0, c_total)
    for n, (part, low, high) in enumerate(blocks):
        got_pair(corr_out.at[1 - core, part, :, pl.ds(low, high - low)], 2 + n)
    for store in stores:
        store.wait()
    for copy in r_copies:
        copy.wait_send()


def finish(
    ka_count, pair_hbm, white_hbm, neighbour_hbm, corr_hbm, whitened_hbm,
    pair_ref, white_ref, neighbour_ref, corr_ref, load_sem, store_sem,
):
    parts = [(d, part) for d in range(2) for part in range(2)]
    order = pltpu.make_async_copy(neighbour_hbm, neighbour_ref, load_sem.at[5])
    order.start()
    loads = [
        pltpu.make_async_copy(pair_hbm.at[d, part], pair_ref.at[d, part], load_sem.at[n])
        for n, (d, part) in enumerate(parts)
    ] + [pltpu.make_async_copy(white_hbm, white_ref, load_sem.at[4])]
    for load in loads:
        load.start()
    order.wait()
    looks_ahead = neighbour_ref[0] == lax.rem(lax.axis_index("ka") + 1, ka_count)
    flip = 1 - looks_ahead.astype(jnp.int32)
    stores = [
        pltpu.make_async_copy(
            corr_ref.at[d, part], corr_hbm.at[d + flip - 2 * d * flip, part], store_sem.at[n]
        )
        for n, (d, part) in enumerate(parts)
    ] + [pltpu.make_async_copy(white_ref, whitened_hbm, store_sem.at[4])]
    for n, (d, part) in enumerate(parts):
        loads[n].wait()
        corr_ref[d, part] = pair_ref[d, part].astype(F32)
        stores[n].start()
    loads[4].wait()
    stores[4].start()
    for store in stores:
        store.wait()


def on_device(ka_count, pw_count, band_coeffs, cutoff_weight, row_order, neighbour, gauge_matrix):
    rows, nb = band_coeffs.shape[2], band_coeffs.shape[3]
    half = nb // CORES
    strips = nb // LANES
    a_rows = half // A_CHUNKS
    c_total = PARTS * strips
    hbm = pl.BlockSpec(memory_space=pltpu.HBM)
    dma = pltpu.SemaphoreType.DMA
    whitened, pair = pl.pallas_call(
        functools.partial(kernel, ka_count, pw_count),
        out_shape=(
            jax.ShapeDtypeStruct((2, rows, nb), BF16),
            jax.ShapeDtypeStruct((2, 2, nb, nb), BF16),
        ),
        in_specs=[hbm] * 4,
        out_specs=(hbm, hbm),
        scratch_shapes=[
            pltpu.VMEM((2, rows, nb), BF16),
            pltpu.VMEM((1, rows), F32),
            pltpu.VMEM((1, rows), jnp.int32),
            pltpu.VMEM((2, nb, nb), BF16),
            pltpu.VMEM((2, rows, nb), BF16),
            dma((8,)),
            pltpu.VMEM((2, rows, nb), BF16),
            pltpu.VMEM((CORES, 2, rows, nb), BF16),
            pltpu.VMEM((nb, CORES * 2 * rows), BF16),
            pltpu.VMEM((CORES, 2, rows, nb), BF16),
            pltpu.VMEM((2, nb, nb), BF16),
            pltpu.VMEM((nb, nb), F32),
            pltpu.VMEM((A_CHUNKS, a_rows, nb), F32),
            pltpu.VMEM((A_CHUNKS, a_rows, nb), BF16),
            pltpu.VMEM((2, A_CHUNKS, a_rows, nb), BF16),
            pltpu.VMEM((A_CHUNKS, a_rows, nb), BF16),
            pltpu.VMEM((A_CHUNKS, a_rows, nb), BF16),
            pltpu.VMEM((strips, 2, nb, LANES), F32),
            pltpu.VMEM((strips, 2, nb, LANES), BF16),
            pltpu.VMEM((2, strips, 2, nb, LANES), BF16),
            pltpu.VMEM((strips, 2, nb, LANES), BF16),
            pltpu.VMEM((CORES, A_CHUNKS, a_rows, nb), BF16),
            pltpu.VMEM((nb, 2 * nb), BF16),
            pltpu.VMEM((nb, 2 * nb), F32),
            pltpu.VMEM((2, nb, nb), BF16),
            dma((5,)),
            dma((5,)),
            dma((strips + U_PIECES,)),
            dma((CORES * (strips + U_PIECES + A_CHUNKS),)),
            dma((CORES, strips)),
            dma((CORES, U_PIECES)),
            dma((A_CHUNKS,)),
            dma((CORES, A_CHUNKS)),
            dma((A_CHUNKS,)),
            dma((2, A_CHUNKS)),
            dma((A_CHUNKS,)),
            dma((A_CHUNKS,)),
            dma((c_total,)),
            dma((2, c_total)),
            dma((c_total,)),
            dma((c_total,)),
        ],
        compiler_params=pltpu.CompilerParams(
            collective_id=0, has_side_effects=True, vmem_limit_bytes=56 << 20
        ),
    )(band_coeffs[0], cutoff_weight, row_order, gauge_matrix[0])
    correlations, whitened = pl.pallas_call(
        functools.partial(finish, ka_count),
        out_shape=(
            jax.ShapeDtypeStruct((2, 2, nb, nb), F32),
            jax.ShapeDtypeStruct((2, rows, nb), BF16),
        ),
        in_specs=[hbm, hbm, hbm],
        out_specs=(hbm, hbm),
        scratch_shapes=[
            pltpu.VMEM((2, 2, nb, nb), BF16),
            pltpu.VMEM((2, rows, nb), BF16),
            pltpu.SMEM((1,), jnp.int32),
            pltpu.VMEM((2, 2, nb, nb), F32),
            dma((6,)),
            dma((5,)),
        ],
        compiler_params=pltpu.CompilerParams(vmem_limit_bytes=56 << 20),
    )(pair, whitened, neighbour)
    return (whitened[None], correlations[None])


def solution(mesh):
    in_specs = (
        P("ka", None, "pw", None),
        P("ka", "pw"),
        P("ka", "pw"),
        P("ka"),
        P("ka", None, None, None),
    )
    out_specs = (P("ka", None, "pw", None), P("ka", None, None, None, None))
    return jax.shard_map(
        functools.partial(on_device, mesh.shape["ka"], mesh.shape["pw"]),
        mesh=mesh, in_specs=in_specs, out_specs=out_specs, check_vma=False,
    )
```

```python
import functools
import math

import jax
import jax.numpy as jnp
from jax import lax
from jax.experimental import pallas as pl
from jax.experimental.pallas import tpu as pltpu
from jax.sharding import PartitionSpec as P

MESH = pl.DeviceIdType.MESH
CORES = 2
LANES = 128
A_CHUNKS = 6
U_PIECES = 2
PARTS = 4
NEAR_STEPS = ((4, 8, 0, 3), (8, 12, 3, 8), (12, 12, 8, 12), (12, 12, 12, 12), (12, 12, 12, 12), (12, 12, 12, 12), (12, 12, 12, 12))
FAR_STEPS = ((0,0,0,0),(0,0,0,0),(0,1,0,0),(1,3,0,0),(3,9,0,3),(9,12,3,6),(12,12,6,12))
F32 = jnp.float32
BF16 = jnp.bfloat16


def mm(left, right):
    return jnp.dot(left, right, preferred_element_type=F32)


def mm_t(left, right):
    return lax.dot_general(left, right, (((0,), (0,)), ((), ())), preferred_element_type=F32)


def complex_mm(left_re, left_im, right_re, right_im):
    width = right_re.shape[1]
    left = jnp.concatenate([left_re, left_im], axis=1)
    right = jnp.concatenate(
        [
            jnp.concatenate([right_re, right_im], axis=1),
            jnp.concatenate([-right_im, right_re], axis=1),
        ],
        axis=0,
    )
    both = mm(left, right)
    return both[:, :width], both[:, width:]


def halves(packed):
    turned = packed.T
    return 0.5 * (packed + turned), 0.5 * (packed - turned)


def kernel(
    ka_count,
    pw_count,
    bands_hbm,
    weight_hbm,
    order_hbm,
    gauge_hbm,
    white_out,
    corr_out,
    bands_ref,
    weight_ref,
    order_ref,
    gauge_ref,
    white_buf,
    load_sem,
    f_buf,
    p_buf,
    own_t,
    fn_buf,
    un_buf,
    a_full,
    a_local,
    a_sum,
    a_in,
    a_tot,
    a_other,
    c_local,
    c_sum,
    c_in,
    c_tot,
    an_buf,
    v_buf,
    x_buf,
    r_buf,
    pair_send,
    pair_recv,
    x_send,
    y_send,
    fn_recv,
    un_recv,
    an_send,
    an_recv,
    a_send,
    a_recv,
    a_out,
    c_send,
    c_recv,
    c_out,
):
    rows, nb = bands_ref.shape[1], bands_ref.shape[2]
    loads = [
        pltpu.make_async_copy(src, dst, load_sem.at[turn])
        for turn, (src, dst) in enumerate(
            [
                (bands_hbm, bands_ref),
                (weight_hbm, weight_ref),
                (order_hbm, order_ref),
                (gauge_hbm, gauge_ref),
            ]
        )
    ]
    for load in loads:
        load.start()
    half = nb // CORES
    strips = nb // LANES
    a_rows = half // A_CHUNKS
    u_rows = nb // U_PIECES
    c_total = PARTS * strips
    k = lax.axis_index("ka")
    p = lax.axis_index("pw")
    core = lax.rem(p, CORES)
    q = lax.div(p, CORES)
    line = pw_count // CORES
    base = q * CORES
    partner = base + 1 - core
    parity = lax.rem(k, 2)
    near = core == parity
    far = core != parity
    across = k + 1 - 2 * parity
    across_core = base + 1 - parity
    onward = lax.rem(k + 2 - 4 * parity + ka_count, ka_count)
    source = lax.rem(k - 2 + 4 * parity + ka_count, ka_count)
    edge = (q == 0) | (q == line - 1)
    inner = jnp.logical_not(edge)
    mid = (q == line // 2 - 1) | (q == line // 2)
    slot = mid.astype(jnp.int32)
    side_sign = jnp.where(2 * q < line, 1, -1)
    inward = p + CORES * side_sign
    outward = p - CORES * side_sign

    barrier = pltpu.get_barrier_semaphore()

    def greet(a, b):
        pl.semaphore_signal(barrier, inc=1, device_id=(a, b), device_id_type=MESH)

    greet(k, partner)
    greet(k, inward)

    @pl.when(near)
    def _():
        for side in range(CORES):
            greet(across, base + side)

    @pl.when(far)
    def _():
        greet(source, partner)

    @pl.when(inner)
    def _():
        greet(k, outward)

    eye = (
        lax.broadcasted_iota(jnp.int32, (nb, nb), 0) == lax.broadcasted_iota(jnp.int32, (nb, nb), 1)
    ).astype(F32)
    first = lax.broadcasted_iota(jnp.int32, (nb, nb), 0) == 0
    rest = jnp.where(first, 0.0, eye)

    for load in loads[:3]:
        load.wait()
    row_id = lax.broadcasted_iota(jnp.int32, (rows, rows), 0)
    col_id = lax.broadcasted_iota(jnp.int32, (rows, rows), 1)
    weight = jnp.sum(jnp.where(row_id == col_id, weight_ref[...], 0.0), axis=1, keepdims=True)
    pick = (row_id == order_ref[...] - p * rows).astype(BF16)
    for part in range(2):
        filtered = (bands_ref[part].astype(F32) * weight).astype(BF16)
        f_buf[part] = filtered
        p_buf[core, part] = mm(pick, filtered).astype(BF16)

    as_one = lambda flag: flag.astype(jnp.int32)
    pl.semaphore_wait(barrier, 3 + as_one(near) + as_one(inner))

    def remote(src, dst, send, recv, a, b):
        return pltpu.make_async_remote_copy(
            src_ref=src, dst_ref=dst, send_sem=send, recv_sem=recv,
            device_id=(a, b), device_id_type=MESH,
        )

    def to_pair(src, dst, turn):
        return remote(src, dst, pair_send.at[turn], pair_recv.at[turn], k, partner)

    def got_pair(dst, turn):
        remote(dst, dst, pair_send.at[turn], pair_recv.at[turn], k, partner).wait_recv()

    def to_across(src, dst, recv, turn):
        return remote(src, dst, x_send.at[turn], recv, across, across_core)

    def arrived(dst, recv):
        remote(dst, dst, x_send.at[0], recv, k, partner).wait_recv()

    def pass_on(dst, recv, turn):
        return remote(dst, dst, y_send.at[turn], recv, onward, partner)

    def strip_of(buf, t):
        return buf.at[:, :, pl.ds(t * LANES, LANES)]

    p_copy = to_pair(p_buf.at[core], p_buf.at[core], 0)
    p_copy.start()
    x_copies = [
        to_across(strip_of(f_buf, t), strip_of(fn_buf.at[core], t), fn_recv.at[core, t], 0)
        for t in range(strips)
    ]
    for copy in x_copies:
        copy.start()
    for load in loads[3:]:
        load.wait()
    u_parts = [(side, piece) for piece in range(U_PIECES) for side in range(CORES)]

    def u_piece(side, piece):
        return un_buf.at[side, pl.ds(piece * u_rows, u_rows)]

    for piece in range(U_PIECES):
        u_copy = to_across(
            gauge_ref.at[core, pl.ds(piece * u_rows, u_rows)], u_piece(core, piece),
            un_recv.at[core, piece], 1,
        )
        u_copy.start()

    f_passed = [
        [
            pass_on(strip_of(fn_buf.at[side], t), fn_recv.at[side, t], 0)
            for side in range(CORES)
        ]
        for t in range(strips)
    ]
    u_passed = [
        pass_on(u_piece(side, piece), un_recv.at[side, piece], 1)
        for side, piece in u_parts
    ]
    n_parts = [(side, i) for i in range(A_CHUNKS) for side in range(CORES)]
    n_passed = [
        pass_on(an_buf.at[side, i], an_recv.at[side, i], 2)
        for side, i in n_parts
    ]

    def pass_a():
        for n, (side, i) in enumerate(n_parts):
            arrived(an_buf.at[side, i], an_recv.at[side, i])
            n_passed[n].start()

    got_pair(p_buf.at[1 - core], 0)
    own_flat = p_buf[...].reshape(CORES * 2 * rows, nb)
    turned = []
    for side in range(CORES):
        turned += [p_buf[side, 1], -p_buf[side, 0]]
    own_turned = jnp.concatenate(turned, axis=0)
    own_t[...] = own_flat.T
    gram = mm(own_t[...], own_flat) + mm(own_t[...], own_turned)
    a_full[...] = gram - (jnp.sum(gram * eye) / nb) * rest
    for i in range(A_CHUNKS):
        a_local[i] = a_full[pl.ds(pl.multiple_of(core * half + i * a_rows, 8), a_rows), :]

    def c_view(buf, i):
        t = lax.div(i, PARTS)
        part = lax.div(lax.rem(i, PARTS), 2)
        low = pl.multiple_of(lax.rem(i, 2) * half, 16)
        return buf.at[t, part, pl.ds(low, half)]

    def a_view(buf, i):
        return buf.at[i]

    def gather(view, local, total, incoming, send, recv, i):
        @pl.when(edge)
        def _():
            view(total, i)[...] = view(local, i)[...].astype(BF16)

        @pl.when(inner)
        def _():
            arrived(view(incoming.at[0], i), recv.at[0, i])
            view(total, i)[...] = (
                view(local, i)[...] + view(incoming.at[0], i)[...].astype(F32)
            ).astype(BF16)

        remote(
            view(total, i), view(incoming.at[slot], i), send.at[0], recv.at[slot, i], k, inward
        ).start()

    def spread(view, total, incoming, final, recv, out, i):
        @pl.when(mid)
        def _():
            arrived(view(incoming.at[1], i), recv.at[1, i])
            view(final, i)[...] = (
                view(total, i)[...].astype(F32) + view(incoming.at[1], i)[...].astype(F32)
            ).astype(BF16)

        @pl.when(jnp.logical_not(mid))
        def _():
            arrived(view(final, i), recv.at[1, i])

        @pl.when(inner)
        def _():
            remote(view(final, i), view(final, i), out.at[0], recv.at[1, i], k, outward).start()

    def gather_a(i):
        gather(a_view, a_local, a_sum, a_in, a_send, a_recv, i)

    def share_a(i):
        return remote(
            a_tot.at[i], an_buf.at[core, i], an_send.at[0], an_recv.at[core, i], across, across_core
        )

    def spread_a(i):
        spread(a_view, a_sum, a_in, a_tot, a_recv, a_out, i)
        share_a(i).start()

    def gather_c(i):
        gather(c_view, c_local, c_sum, c_in, c_send, c_recv, i)

    def spread_c(i):
        spread(c_view, c_sum, c_in, c_tot, c_recv, c_out, i)

    def over(one, start, stop):
        def step(i, carry):
            one(i)
            return carry

        lax.fori_loop(start, stop, step, 0)

    def at_cut(cut):
        return cut * c_total // 12

    def sums(turn):
        bounds = [
            jnp.where(near, at_cut(a), at_cut(b)) for a, b in zip(NEAR_STEPS[turn], FAR_STEPS[turn])
        ]
        g_low, g_high, s_low, s_high = bounds

        @pl.when(inner)
        def _():
            def one(n):
                @pl.when(g_low + n < g_high)
                def _():
                    gather_c(g_low + n)

                @pl.when(s_low + n < s_high)
                def _():
                    spread_c(s_low + n)

            over(one, 0, jnp.maximum(g_high - g_low, s_high - s_low))

    a_copy = to_pair(a_tot, a_other, 1)

    def get_strip(t, forward):
        for side in range(CORES):
            arrived(strip_of(fn_buf.at[side], t), fn_recv.at[side, t])
            if forward:
                f_passed[t][side].start()

    def cross_strip(t):
        low, high = t * LANES, (t + 1) * LANES
        plain, other = [], []
        for side in range(CORES):
            re, im = fn_buf[side, 0, :, low:high], fn_buf[side, 1, :, low:high]
            plain += [re, im]
            other += [im, -re]
        right = jnp.concatenate(
            [jnp.concatenate(plain, axis=0), jnp.concatenate(other, axis=0)], axis=1
        )
        cross = mm(own_t[...], right)
        c_local[t, 0] = cross[:, :LANES]
        c_local[t, 1] = cross[:, LANES:]

    def edge_strip(t):
        @pl.when(edge)
        def _():
            over(gather_c, PARTS * t, PARTS * (t + 1))

    def pass_u(piece):
        for n, (side, own) in enumerate(u_parts):
            if own == piece:
                arrived(u_piece(side, piece), un_recv.at[side, piece])
                u_passed[n].start()

    @pl.when(edge)
    def _():
        over(gather_a, 0, A_CHUNKS)

    a_cuts = [A_CHUNKS * t // strips for t in range(strips + 1)]

    @pl.when(near)
    def _():
        for t in range(strips):
            get_strip(t, True)

            @pl.when(inner)
            def _():
                over(gather_a, a_cuts[t], a_cuts[t + 1])

            cross_strip(t)
            edge_strip(t)

        @pl.when(inner)
        def _():
            over(gather_c, 0, at_cut(2))
            over(spread_a, 0, A_CHUNKS // 2)
            over(gather_c, at_cut(2), at_cut(4))
            over(spread_a, A_CHUNKS // 2, A_CHUNKS)
            a_copy.start()
            pass_u(0)
            sums(0)

    @pl.when(far)
    def _():
        @pl.when(inner)
        def _():
            over(gather_a, 0, A_CHUNKS)
            over(spread_a, 0, A_CHUNKS)
            a_copy.start()

        for t in range(strips):
            get_strip(t, False)
            cross_strip(t)
            edge_strip(t)

    @pl.when(edge)
    def _():
        @pl.when(near)
        def _():
            for piece in range(U_PIECES):
                pass_u(piece)

        over(spread_a, 0, A_CHUNKS)
        a_copy.start()
        pl.when(near)(pass_a)

    @pl.when(near & inner)
    def _():
        for piece in range(1, U_PIECES):
            pass_u(piece)

    sums(1)
    pl.when(near & inner)(pass_a)
    sums(2)
    got_pair(a_other, 1)
    a_full[pl.ds(pl.multiple_of(core * half, 8), half), :] = (
        a_tot[...].astype(F32).reshape(half, nb)
    )
    a_full[pl.ds(pl.multiple_of((1 - core) * half, 8), half), :] = (
        a_other[...].astype(F32).reshape(half, nb)
    )

    def newton(packed, between):
        mean = jnp.sum(packed * eye)
        deviation = packed - mean * (eye - rest)
        e_re, e_im = halves(deviation * (0.5 / mean))
        e_re_b, e_im_b = e_re.astype(BF16), e_im.astype(BF16)
        sq_re, sq_im = complex_mm(e_re_b, e_im_b, e_re_b, e_im_b)
        between()
        left_re, left_im = e_re - 0.5 * sq_re, e_im - 0.5 * sq_im
        right_re, right_im = 0.25 * sq_re - 1.25 * e_re, 0.25 * sq_im - 1.25 * e_im
        last_re, last_im = complex_mm(
            left_re.astype(BF16), left_im.astype(BF16), right_re.astype(BF16), right_im.astype(BF16)
        )
        white_re = (
            1.38671875 * eye - 0.75 * e_re - 0.78125 * left_re - 0.3125 * right_re - 0.5 * last_re
        )
        white_im = -0.75 * e_im - 0.78125 * left_im - 0.3125 * right_im - 0.5 * last_im
        return white_re.astype(BF16), white_im.astype(BF16)

    w_re, w_im = newton(a_full[...], lambda: sums(3))
    sums(4)
    out_re, out_im = complex_mm(f_buf[0], f_buf[1], w_re, w_im)
    white_buf[0] = out_re.astype(BF16)
    white_buf[1] = out_im.astype(BF16)
    stores = [pltpu.make_async_copy(white_buf, white_out, load_sem.at[4])]
    stores[0].start()
    sums(5)
    root = math.sqrt(rows * pw_count)
    v_re = mm_t(gauge_ref[0], w_re) + mm_t(gauge_ref[1], w_im)
    v_im = mm_t(gauge_ref[0], w_im) - mm_t(gauge_ref[1], w_re)
    v_buf[:, :nb] = (v_re * root).astype(BF16)
    v_buf[:, nb:] = (v_im * root).astype(BF16)
    sums(6)

    @pl.when(far)
    def _():
        for side, piece in u_parts:
            arrived(u_piece(side, piece), un_recv.at[side, piece])
        for side, i in n_parts:
            arrived(an_buf.at[side, i], an_recv.at[side, i])

    next_re, next_im = newton(an_buf[...].astype(F32).reshape(nb, nb), lambda: None)
    vn_re, vn_im = complex_mm(next_re, next_im, un_buf[0], un_buf[1])
    vn_re, vn_im = vn_re.astype(BF16), vn_im.astype(BF16)
    moved = None
    for low, high in ((0, strips - 1), (strips - 1, strips)):
        @pl.when(edge)
        def _():
            over(spread_c, PARTS * low, PARTS * high)

        left = jnp.concatenate(
            [c_tot[t, part] for part in range(2) for t in range(low, high)], axis=1
        )
        re, im = vn_re[low * LANES : high * LANES], vn_im[low * LANES : high * LANES]
        right = jnp.concatenate(
            [jnp.concatenate([re, im], axis=1), jnp.concatenate([-im, re], axis=1)], axis=0
        )
        if low == 0:
            x_buf[...] = mm(left, right)
        else:
            moved = x_buf[...] + mm(left, right)
    x_re, x_im = moved[:, :nb].astype(BF16), moved[:, nb:].astype(BF16)
    right = jnp.concatenate(
        [jnp.concatenate([x_re, x_im], axis=1), jnp.concatenate([-x_im, x_re], axis=1)], axis=0
    )
    blocks = [(0, 0, nb), (1, 0, nb - 2 * LANES), (1, nb - 2 * LANES, nb)]
    r_copies = []
    for n, (part, low, high) in enumerate(blocks):
        cols = pl.ds(low, high - low)
        own, there = r_buf.at[part, :, cols], corr_out.at[core, part, :, cols]
        r_copies.append(to_pair(own, there, 2 + n))
        stores.append(pltpu.make_async_copy(own, there, load_sem.at[5 + n]))
    edge_col = 2 * nb - 2 * LANES
    result = mm(v_buf[...], right[:, :edge_col])
    r_buf[0] = result[:, :nb].astype(BF16)
    r_copies[0].start()
    stores[1].start()
    r_buf[1, :, : nb - 2 * LANES] = result[:, nb:].astype(BF16)
    r_copies[1].start()
    stores[2].start()
    r_buf[1, :, nb - 2 * LANES :] = mm(v_buf[...], right[:, edge_col:]).astype(BF16)
    r_copies[2].start()
    stores[3].start()

    def all_sent(buf, send):
        remote(buf, buf, send, pair_recv.at[0], k, partner).wait_send()

    for copy in [p_copy, a_copy]:
        copy.wait_send()
    all_sent(f_buf, x_send.at[0])
    all_sent(gauge_ref.at[core], x_send.at[1])
    all_sent(a_tot, an_send.at[0])
    all_sent(a_sum, a_send.at[0])
    all_sent(c_sum, c_send.at[0])

    @pl.when(near)
    def _():
        for turn, buf in enumerate((fn_buf, un_buf, an_buf)):
            all_sent(buf, y_send.at[turn])

    @pl.when(inner)
    def _():
        all_sent(a_tot, a_out.at[0])
        all_sent(c_tot, c_out.at[0])

    for n, (part, low, high) in enumerate(blocks):
        got_pair(corr_out.at[1 - core, part, :, pl.ds(low, high - low)], 2 + n)
    for store in stores:
        store.wait()
    for copy in r_copies:
        copy.wait_send()


def finish(
    ka_count, pair_hbm, white_hbm, neighbour_hbm, corr_hbm, whitened_hbm,
    pair_ref, white_ref, neighbour_ref, corr_ref, load_sem, store_sem,
):
    parts = [(d, part) for d in range(2) for part in range(2)]
    order = pltpu.make_async_copy(neighbour_hbm, neighbour_ref, load_sem.at[5])
    order.start()
    loads = [
        pltpu.make_async_copy(pair_hbm.at[d, part], pair_ref.at[d, part], load_sem.at[n])
        for n, (d, part) in enumerate(parts)
    ] + [pltpu.make_async_copy(white_hbm, white_ref, load_sem.at[4])]
    for load in loads:
        load.start()
    order.wait()
    looks_ahead = neighbour_ref[0] == lax.rem(lax.axis_index("ka") + 1, ka_count)
    flip = 1 - looks_ahead.astype(jnp.int32)
    stores = [
        pltpu.make_async_copy(
            corr_ref.at[d, part], corr_hbm.at[d + flip - 2 * d * flip, part], store_sem.at[n]
        )
        for n, (d, part) in enumerate(parts)
    ] + [pltpu.make_async_copy(white_ref, whitened_hbm, store_sem.at[4])]
    for n, (d, part) in enumerate(parts):
        loads[n].wait()
        corr_ref[d, part] = pair_ref[d, part].astype(F32)
        stores[n].start()
    loads[4].wait()
    stores[4].start()
    for store in stores:
        store.wait()


def on_device(ka_count, pw_count, band_coeffs, cutoff_weight, row_order, neighbour, gauge_matrix):
    rows, nb = band_coeffs.shape[2], band_coeffs.shape[3]
    half = nb // CORES
    strips = nb // LANES
    a_rows = half // A_CHUNKS
    c_total = PARTS * strips
    hbm = pl.BlockSpec(memory_space=pltpu.HBM)
    dma = pltpu.SemaphoreType.DMA
    whitened, pair = pl.pallas_call(
        functools.partial(kernel, ka_count, pw_count),
        out_shape=(
            jax.ShapeDtypeStruct((2, rows, nb), BF16),
            jax.ShapeDtypeStruct((2, 2, nb, nb), BF16),
        ),
        in_specs=[hbm] * 4,
        out_specs=(hbm, hbm),
        scratch_shapes=[
            pltpu.VMEM((2, rows, nb), BF16),
            pltpu.VMEM((1, rows), F32),
            pltpu.VMEM((1, rows), jnp.int32),
            pltpu.VMEM((2, nb, nb), BF16),
            pltpu.VMEM((2, rows, nb), BF16),
            dma((8,)),
            pltpu.VMEM((2, rows, nb), BF16),
            pltpu.VMEM((CORES, 2, rows, nb), BF16),
            pltpu.VMEM((nb, CORES * 2 * rows), BF16),
            pltpu.VMEM((CORES, 2, rows, nb), BF16),
            pltpu.VMEM((2, nb, nb), BF16),
            pltpu.VMEM((nb, nb), F32),
            pltpu.VMEM((A_CHUNKS, a_rows, nb), F32),
            pltpu.VMEM((A_CHUNKS, a_rows, nb), BF16),
            pltpu.VMEM((2, A_CHUNKS, a_rows, nb), BF16),
            pltpu.VMEM((A_CHUNKS, a_rows, nb), BF16),
            pltpu.VMEM((A_CHUNKS, a_rows, nb), BF16),
            pltpu.VMEM((strips, 2, nb, LANES), F32),
            pltpu.VMEM((strips, 2, nb, LANES), BF16),
            pltpu.VMEM((2, strips, 2, nb, LANES), BF16),
            pltpu.VMEM((strips, 2, nb, LANES), BF16),
            pltpu.VMEM((CORES, A_CHUNKS, a_rows, nb), BF16),
            pltpu.VMEM((nb, 2 * nb), BF16),
            pltpu.VMEM((nb, 2 * nb), F32),
            pltpu.VMEM((2, nb, nb), BF16),
            dma((5,)),
            dma((5,)),
            dma((2,)),
            dma((3,)),
            dma((CORES, strips)),
            dma((CORES, U_PIECES)),
            dma((1,)),
            dma((CORES, A_CHUNKS)),
            dma((1,)),
            dma((2, A_CHUNKS)),
            dma((1,)),
            dma((1,)),
            dma((2, c_total)),
            dma((1,)),
        ],
        compiler_params=pltpu.CompilerParams(
            collective_id=0, has_side_effects=True, vmem_limit_bytes=56 << 20
        ),
    )(band_coeffs[0], cutoff_weight, row_order, gauge_matrix[0])
    correlations, whitened = pl.pallas_call(
        functools.partial(finish, ka_count),
        out_shape=(
            jax.ShapeDtypeStruct((2, 2, nb, nb), F32),
            jax.ShapeDtypeStruct((2, rows, nb), BF16),
        ),
        in_specs=[hbm, hbm, hbm],
        out_specs=(hbm, hbm),
        scratch_shapes=[
            pltpu.VMEM((2, 2, nb, nb), BF16),
            pltpu.VMEM((2, rows, nb), BF16),
            pltpu.SMEM((1,), jnp.int32),
            pltpu.VMEM((2, 2, nb, nb), F32),
            dma((6,)),
            dma((5,)),
        ],
        compiler_params=pltpu.CompilerParams(vmem_limit_bytes=56 << 20),
    )(pair, whitened, neighbour)
    return (whitened[None], correlations[None])


def solution(mesh):
    in_specs = (
        P("ka", None, "pw", None),
        P("ka", "pw"),
        P("ka", "pw"),
        P("ka"),
        P("ka", None, None, None),
    )
    out_specs = (P("ka", None, "pw", None), P("ka", None, None, None, None))
    return jax.shard_map(
        functools.partial(on_device, mesh.shape["ka"], mesh.shape["pw"]),
        mesh=mesh, in_specs=in_specs, out_specs=out_specs, check_vma=False,
    )
```

```python
import functools
import math

import jax
import jax.numpy as jnp
from jax import lax
from jax.experimental import pallas as pl
from jax.experimental.pallas import tpu as pltpu
from jax.sharding import PartitionSpec as P

MESH = pl.DeviceIdType.MESH
CORES = 2
LANES = 128
A_CHUNKS = 6
U_PIECES = 3
PARTS = 4
NEAR_STEPS = ((4, 8, 0, 3), (8, 12, 3, 8), (12, 12, 8, 12), (12, 12, 12, 12), (12, 12, 12, 12), (12, 12, 12, 12), (12, 12, 12, 12))
FAR_STEPS = ((0,0,0,0),(0,1,0,0),(1,2,0,0),(2,4,0,0),(4,10,0,4),(10,12,4,7),(12,12,7,12))
F32 = jnp.float32
BF16 = jnp.bfloat16


def mm(left, right):
    return jnp.dot(left, right, preferred_element_type=F32)


def mm_t(left, right):
    return lax.dot_general(left, right, (((0,), (0,)), ((), ())), preferred_element_type=F32)


def complex_mm(left_re, left_im, right_re, right_im):
    width = right_re.shape[1]
    left = jnp.concatenate([left_re, left_im], axis=1)
    right = jnp.concatenate(
        [
            jnp.concatenate([right_re, right_im], axis=1),
            jnp.concatenate([-right_im, right_re], axis=1),
        ],
        axis=0,
    )
    both = mm(left, right)
    return both[:, :width], both[:, width:]


def halves(packed):
    turned = packed.T
    return 0.5 * (packed + turned), 0.5 * (packed - turned)


def kernel(
    ka_count,
    pw_count,
    bands_hbm,
    weight_hbm,
    order_hbm,
    gauge_hbm,
    white_out,
    corr_out,
    bands_ref,
    weight_ref,
    order_ref,
    gauge_ref,
    white_buf,
    load_sem,
    f_buf,
    p_buf,
    own_t,
    fn_buf,
    un_buf,
    a_full,
    a_local,
    a_sum,
    a_in,
    a_tot,
    a_other,
    c_local,
    c_sum,
    c_in,
    c_tot,
    an_buf,
    v_buf,
    x_buf,
    r_buf,
    pair_send,
    pair_recv,
    x_send,
    y_send,
    fn_recv,
    un_recv,
    an_send,
    an_recv,
    a_send,
    a_recv,
    a_out,
    c_send,
    c_recv,
    c_out,
):
    rows, nb = bands_ref.shape[1], bands_ref.shape[2]
    loads = [
        pltpu.make_async_copy(src, dst, load_sem.at[turn])
        for turn, (src, dst) in enumerate(
            [
                (bands_hbm, bands_ref),
                (weight_hbm, weight_ref),
                (order_hbm, order_ref),
                (gauge_hbm, gauge_ref),
            ]
        )
    ]
    for load in loads:
        load.start()
    half = nb // CORES
    strips = nb // LANES
    a_rows = half // A_CHUNKS
    u_rows = nb // U_PIECES
    c_total = PARTS * strips
    k = lax.axis_index("ka")
    p = lax.axis_index("pw")
    core = lax.rem(p, CORES)
    q = lax.div(p, CORES)
    line = pw_count // CORES
    base = q * CORES
    partner = base + 1 - core
    parity = lax.rem(k, 2)
    near = core == parity
    far = core != parity
    across = k + 1 - 2 * parity
    across_core = base + 1 - parity
    onward = lax.rem(k + 2 - 4 * parity + ka_count, ka_count)
    source = lax.rem(k - 2 + 4 * parity + ka_count, ka_count)
    edge = (q == 0) | (q == line - 1)
    inner = jnp.logical_not(edge)
    mid = (q == line // 2 - 1) | (q == line // 2)
    slot = mid.astype(jnp.int32)
    side_sign = jnp.where(2 * q < line, 1, -1)
    inward = p + CORES * side_sign
    outward = p - CORES * side_sign

    barrier = pltpu.get_barrier_semaphore()

    def greet(a, b):
        pl.semaphore_signal(barrier, inc=1, device_id=(a, b), device_id_type=MESH)

    greet(k, partner)
    greet(k, inward)

    @pl.when(near)
    def _():
        for side in range(CORES):
            greet(across, base + side)

    @pl.when(far)
    def _():
        greet(source, partner)

    @pl.when(inner)
    def _():
        greet(k, outward)

    eye = (
        lax.broadcasted_iota(jnp.int32, (nb, nb), 0) == lax.broadcasted_iota(jnp.int32, (nb, nb), 1)
    ).astype(F32)
    first = lax.broadcasted_iota(jnp.int32, (nb, nb), 0) == 0
    rest = jnp.where(first, 0.0, eye)

    for load in loads[:3]:
        load.wait()
    row_id = lax.broadcasted_iota(jnp.int32, (rows, rows), 0)
    col_id = lax.broadcasted_iota(jnp.int32, (rows, rows), 1)
    weight = jnp.sum(jnp.where(row_id == col_id, weight_ref[...], 0.0), axis=1, keepdims=True)
    pick = (row_id == order_ref[...] - p * rows).astype(BF16)
    for part in range(2):
        filtered = (bands_ref[part].astype(F32) * weight).astype(BF16)
        f_buf[part] = filtered
        p_buf[core, part] = mm(pick, filtered).astype(BF16)

    as_one = lambda flag: flag.astype(jnp.int32)
    pl.semaphore_wait(barrier, 3 + as_one(near) + as_one(inner))

    def remote(src, dst, send, recv, a, b):
        return pltpu.make_async_remote_copy(
            src_ref=src, dst_ref=dst, send_sem=send, recv_sem=recv,
            device_id=(a, b), device_id_type=MESH,
        )

    def to_pair(src, dst, turn):
        return remote(src, dst, pair_send.at[turn], pair_recv.at[turn], k, partner)

    def got_pair(dst, turn):
        remote(dst, dst, pair_send.at[turn], pair_recv.at[turn], k, partner).wait_recv()

    def to_across(src, dst, recv, turn):
        return remote(src, dst, x_send.at[turn], recv, across, across_core)

    def arrived(dst, recv):
        remote(dst, dst, x_send.at[0], recv, k, partner).wait_recv()

    def pass_on(dst, recv, turn):
        return remote(dst, dst, y_send.at[turn], recv, onward, partner)

    def strip_of(buf, t):
        return buf.at[:, :, pl.ds(t * LANES, LANES)]

    p_copy = to_pair(p_buf.at[core], p_buf.at[core], 0)
    p_copy.start()
    x_copies = [
        to_across(strip_of(f_buf, t), strip_of(fn_buf.at[core], t), fn_recv.at[core, t], 0)
        for t in range(strips)
    ]
    for copy in x_copies:
        copy.start()
    for load in loads[3:]:
        load.wait()
    u_parts = [(side, piece) for piece in range(U_PIECES) for side in range(CORES)]

    def u_piece(side, piece):
        return un_buf.at[side, pl.ds(piece * u_rows, u_rows)]

    for piece in range(U_PIECES):
        u_copy = to_across(
            gauge_ref.at[core, pl.ds(piece * u_rows, u_rows)], u_piece(core, piece),
            un_recv.at[core, piece], 1,
        )
        u_copy.start()

    f_passed = [
        [
            pass_on(strip_of(fn_buf.at[side], t), fn_recv.at[side, t], 0)
            for side in range(CORES)
        ]
        for t in range(strips)
    ]
    u_passed = [
        pass_on(u_piece(side, piece), un_recv.at[side, piece], 1)
        for side, piece in u_parts
    ]
    n_parts = [(side, i) for i in range(A_CHUNKS) for side in range(CORES)]
    n_passed = [
        pass_on(an_buf.at[side, i], an_recv.at[side, i], 2)
        for side, i in n_parts
    ]

    def pass_a():
        for n, (side, i) in enumerate(n_parts):
            arrived(an_buf.at[side, i], an_recv.at[side, i])
            n_passed[n].start()

    got_pair(p_buf.at[1 - core], 0)
    own_flat = p_buf[...].reshape(CORES * 2 * rows, nb)
    turned = []
    for side in range(CORES):
        turned += [p_buf[side, 1], -p_buf[side, 0]]
    own_turned = jnp.concatenate(turned, axis=0)
    own_t[...] = own_flat.T
    gram = mm(own_t[...], own_flat) + mm(own_t[...], own_turned)
    a_full[...] = gram - (jnp.sum(gram * eye) / nb) * rest
    for i in range(A_CHUNKS):
        a_local[i] = a_full[pl.ds(pl.multiple_of(core * half + i * a_rows, 8), a_rows), :]

    def c_view(buf, i):
        t = lax.div(i, PARTS)
        part = lax.div(lax.rem(i, PARTS), 2)
        low = pl.multiple_of(lax.rem(i, 2) * half, 16)
        return buf.at[t, part, pl.ds(low, half)]

    def a_view(buf, i):
        return buf.at[i]

    def gather(view, local, total, incoming, send, recv, i):
        @pl.when(edge)
        def _():
            view(total, i)[...] = view(local, i)[...].astype(BF16)

        @pl.when(inner)
        def _():
            arrived(view(incoming.at[0], i), recv.at[0, i])
            view(total, i)[...] = (
                view(local, i)[...] + view(incoming.at[0], i)[...].astype(F32)
            ).astype(BF16)

        remote(
            view(total, i), view(incoming.at[slot], i), send.at[0], recv.at[slot, i], k, inward
        ).start()

    def spread(view, total, incoming, final, recv, out, i):
        @pl.when(mid)
        def _():
            arrived(view(incoming.at[1], i), recv.at[1, i])
            view(final, i)[...] = (
                view(total, i)[...].astype(F32) + view(incoming.at[1], i)[...].astype(F32)
            ).astype(BF16)

        @pl.when(jnp.logical_not(mid))
        def _():
            arrived(view(final, i), recv.at[1, i])

        @pl.when(inner)
        def _():
            remote(view(final, i), view(final, i), out.at[0], recv.at[1, i], k, outward).start()

    def gather_a(i):
        gather(a_view, a_local, a_sum, a_in, a_send, a_recv, i)

    def share_a(i):
        return remote(
            a_tot.at[i], an_buf.at[core, i], an_send.at[0], an_recv.at[core, i], across, across_core
        )

    def spread_a(i):
        spread(a_view, a_sum, a_in, a_tot, a_recv, a_out, i)
        share_a(i).start()

    def gather_c(i):
        gather(c_view, c_local, c_sum, c_in, c_send, c_recv, i)

    def spread_c(i):
        spread(c_view, c_sum, c_in, c_tot, c_recv, c_out, i)

    def over(one, start, stop):
        def step(i, carry):
            one(i)
            return carry

        lax.fori_loop(start, stop, step, 0)

    def at_cut(cut):
        return cut * c_total // 12

    def sums(turn):
        bounds = [
            jnp.where(near, at_cut(a), at_cut(b)) for a, b in zip(NEAR_STEPS[turn], FAR_STEPS[turn])
        ]
        g_low, g_high, s_low, s_high = bounds

        @pl.when(inner)
        def _():
            def one(n):
                @pl.when(g_low + n < g_high)
                def _():
                    gather_c(g_low + n)

                @pl.when(s_low + n < s_high)
                def _():
                    spread_c(s_low + n)

            over(one, 0, jnp.maximum(g_high - g_low, s_high - s_low))

    a_copy = to_pair(a_tot, a_other, 1)

    def get_strip(t, forward):
        for side in range(CORES):
            arrived(strip_of(fn_buf.at[side], t), fn_recv.at[side, t])
            if forward:
                f_passed[t][side].start()

    def cross_strip(t):
        low, high = t * LANES, (t + 1) * LANES
        plain, other = [], []
        for side in range(CORES):
            re, im = fn_buf[side, 0, :, low:high], fn_buf[side, 1, :, low:high]
            plain += [re, im]
            other += [im, -re]
        right = jnp.concatenate(
            [jnp.concatenate(plain, axis=0), jnp.concatenate(other, axis=0)], axis=1
        )
        cross = mm(own_t[...], right)
        c_local[t, 0] = cross[:, :LANES]
        c_local[t, 1] = cross[:, LANES:]

    def edge_strip(t):
        @pl.when(edge)
        def _():
            over(gather_c, PARTS * t, PARTS * (t + 1))

    def pass_u(piece):
        for n, (side, own) in enumerate(u_parts):
            if own == piece:
                arrived(u_piece(side, piece), un_recv.at[side, piece])
                u_passed[n].start()

    @pl.when(edge)
    def _():
        over(gather_a, 0, A_CHUNKS)

    a_cuts = [A_CHUNKS * t // strips for t in range(strips + 1)]

    @pl.when(near)
    def _():
        for t in range(strips):
            get_strip(t, True)

            @pl.when(inner)
            def _():
                over(gather_a, a_cuts[t], a_cuts[t + 1])

            cross_strip(t)
            edge_strip(t)

        @pl.when(inner)
        def _():
            over(gather_c, 0, at_cut(2))
            over(spread_a, 0, A_CHUNKS // 2)
            over(gather_c, at_cut(2), at_cut(4))
            over(spread_a, A_CHUNKS // 2, A_CHUNKS)
            a_copy.start()
            pass_u(0)
            sums(0)

    @pl.when(far)
    def _():
        @pl.when(inner)
        def _():
            over(gather_a, 0, A_CHUNKS)
            over(spread_a, 0, A_CHUNKS)
            a_copy.start()

        for t in range(strips):
            get_strip(t, False)
            cross_strip(t)
            edge_strip(t)

    @pl.when(edge)
    def _():
        @pl.when(near)
        def _():
            for piece in range(U_PIECES):
                pass_u(piece)

        over(spread_a, 0, A_CHUNKS)
        a_copy.start()
        pl.when(near)(pass_a)

    @pl.when(near & inner)
    def _():
        for piece in range(1, U_PIECES):
            pass_u(piece)

    sums(1)
    pl.when(near & inner)(pass_a)
    sums(2)
    got_pair(a_other, 1)
    a_full[pl.ds(pl.multiple_of(core * half, 8), half), :] = (
        a_tot[...].astype(F32).reshape(half, nb)
    )
    a_full[pl.ds(pl.multiple_of((1 - core) * half, 8), half), :] = (
        a_other[...].astype(F32).reshape(half, nb)
    )

    def newton(packed, between):
        mean = jnp.sum(packed * eye)
        deviation = packed - mean * (eye - rest)
        e_re, e_im = halves(deviation * (0.5 / mean))
        e_re_b, e_im_b = e_re.astype(BF16), e_im.astype(BF16)
        sq_re, sq_im = complex_mm(e_re_b, e_im_b, e_re_b, e_im_b)
        between()
        left_re, left_im = e_re - 0.5 * sq_re, e_im - 0.5 * sq_im
        right_re, right_im = 0.25 * sq_re - 1.25 * e_re, 0.25 * sq_im - 1.25 * e_im
        last_re, last_im = complex_mm(
            left_re.astype(BF16), left_im.astype(BF16), right_re.astype(BF16), right_im.astype(BF16)
        )
        white_re = (
            1.38671875 * eye - 0.75 * e_re - 0.78125 * left_re - 0.3125 * right_re - 0.5 * last_re
        )
        white_im = -0.75 * e_im - 0.78125 * left_im - 0.3125 * right_im - 0.5 * last_im
        return white_re.astype(BF16), white_im.astype(BF16)

    w_re, w_im = newton(a_full[...], lambda: sums(3))
    sums(4)
    out_re, out_im = complex_mm(f_buf[0], f_buf[1], w_re, w_im)
    white_buf[0] = out_re.astype(BF16)
    white_buf[1] = out_im.astype(BF16)
    stores = [pltpu.make_async_copy(white_buf, white_out, load_sem.at[4])]
    stores[0].start()
    sums(5)
    root = math.sqrt(rows * pw_count)
    v_re = mm_t(gauge_ref[0], w_re) + mm_t(gauge_ref[1], w_im)
    v_im = mm_t(gauge_ref[0], w_im) - mm_t(gauge_ref[1], w_re)
    v_buf[:, :nb] = (v_re * root).astype(BF16)
    v_buf[:, nb:] = (v_im * root).astype(BF16)
    sums(6)

    @pl.when(far)
    def _():
        for side, piece in u_parts:
            arrived(u_piece(side, piece), un_recv.at[side, piece])
        for side, i in n_parts:
            arrived(an_buf.at[side, i], an_recv.at[side, i])

    next_re, next_im = newton(an_buf[...].astype(F32).reshape(nb, nb), lambda: None)
    vn_re, vn_im = complex_mm(next_re, next_im, un_buf[0], un_buf[1])
    vn_re, vn_im = vn_re.astype(BF16), vn_im.astype(BF16)
    moved = None
    for low, high in ((0, strips - 1), (strips - 1, strips)):
        @pl.when(edge)
        def _():
            over(spread_c, PARTS * low, PARTS * high)

        left = jnp.concatenate(
            [c_tot[t, part] for part in range(2) for t in range(low, high)], axis=1
        )
        re, im = vn_re[low * LANES : high * LANES], vn_im[low * LANES : high * LANES]
        right = jnp.concatenate(
            [jnp.concatenate([re, im], axis=1), jnp.concatenate([-im, re], axis=1)], axis=0
        )
        if low == 0:
            x_buf[...] = mm(left, right)
        else:
            moved = x_buf[...] + mm(left, right)
    x_re, x_im = moved[:, :nb].astype(BF16), moved[:, nb:].astype(BF16)
    right = jnp.concatenate(
        [jnp.concatenate([x_re, x_im], axis=1), jnp.concatenate([-x_im, x_re], axis=1)], axis=0
    )
    blocks = [(0, 0, nb), (1, 0, nb - 2 * LANES), (1, nb - 2 * LANES, nb)]
    r_copies = []
    for n, (part, low, high) in enumerate(blocks):
        cols = pl.ds(low, high - low)
        own, there = r_buf.at[part, :, cols], corr_out.at[core, part, :, cols]
        r_copies.append(to_pair(own, there, 2 + n))
        stores.append(pltpu.make_async_copy(own, there, load_sem.at[5 + n]))
    edge_col = 2 * nb - 2 * LANES
    result = mm(v_buf[...], right[:, :edge_col])
    r_buf[0] = result[:, :nb].astype(BF16)
    r_copies[0].start()
    stores[1].start()
    r_buf[1, :, : nb - 2 * LANES] = result[:, nb:].astype(BF16)
    r_copies[1].start()
    stores[2].start()
    r_buf[1, :, nb - 2 * LANES :] = mm(v_buf[...], right[:, edge_col:]).astype(BF16)
    r_copies[2].start()
    stores[3].start()

    def all_sent(buf, send):
        remote(buf, buf, send, pair_recv.at[0], k, partner).wait_send()

    for copy in [p_copy, a_copy]:
        copy.wait_send()
    all_sent(f_buf, x_send.at[0])
    all_sent(gauge_ref.at[core], x_send.at[1])
    all_sent(a_tot, an_send.at[0])
    all_sent(a_sum, a_send.at[0])
    all_sent(c_sum, c_send.at[0])

    @pl.when(near)
    def _():
        for turn, buf in enumerate((fn_buf, un_buf, an_buf)):
            all_sent(buf, y_send.at[turn])

    @pl.when(inner)
    def _():
        all_sent(a_tot, a_out.at[0])
        all_sent(c_tot, c_out.at[0])

    for n, (part, low, high) in enumerate(blocks):
        got_pair(corr_out.at[1 - core, part, :, pl.ds(low, high - low)], 2 + n)
    for store in stores:
        store.wait()
    for copy in r_copies:
        copy.wait_send()


def finish(
    ka_count, pair_hbm, white_hbm, neighbour_hbm, corr_hbm, whitened_hbm,
    pair_ref, white_ref, neighbour_ref, corr_ref, load_sem, store_sem,
):
    parts = [(d, part) for d in range(2) for part in range(2)]
    order = pltpu.make_async_copy(neighbour_hbm, neighbour_ref, load_sem.at[5])
    order.start()
    loads = [
        pltpu.make_async_copy(pair_hbm.at[d, part], pair_ref.at[d, part], load_sem.at[n])
        for n, (d, part) in enumerate(parts)
    ] + [pltpu.make_async_copy(white_hbm, white_ref, load_sem.at[4])]
    for load in loads:
        load.start()
    order.wait()
    looks_ahead = neighbour_ref[0] == lax.rem(lax.axis_index("ka") + 1, ka_count)
    flip = 1 - looks_ahead.astype(jnp.int32)
    stores = [
        pltpu.make_async_copy(
            corr_ref.at[d, part], corr_hbm.at[d + flip - 2 * d * flip, part], store_sem.at[n]
        )
        for n, (d, part) in enumerate(parts)
    ] + [pltpu.make_async_copy(white_ref, whitened_hbm, store_sem.at[4])]
    for n, (d, part) in enumerate(parts):
        loads[n].wait()
        corr_ref[d, part] = pair_ref[d, part].astype(F32)
        stores[n].start()
    loads[4].wait()
    stores[4].start()
    for store in stores:
        store.wait()


def on_device(ka_count, pw_count, band_coeffs, cutoff_weight, row_order, neighbour, gauge_matrix):
    rows, nb = band_coeffs.shape[2], band_coeffs.shape[3]
    half = nb // CORES
    strips = nb // LANES
    a_rows = half // A_CHUNKS
    c_total = PARTS * strips
    hbm = pl.BlockSpec(memory_space=pltpu.HBM)
    dma = pltpu.SemaphoreType.DMA
    whitened, pair = pl.pallas_call(
        functools.partial(kernel, ka_count, pw_count),
        out_shape=(
            jax.ShapeDtypeStruct((2, rows, nb), BF16),
            jax.ShapeDtypeStruct((2, 2, nb, nb), BF16),
        ),
        in_specs=[hbm] * 4,
        out_specs=(hbm, hbm),
        scratch_shapes=[
            pltpu.VMEM((2, rows, nb), BF16),
            pltpu.VMEM((1, rows), F32),
            pltpu.VMEM((1, rows), jnp.int32),
            pltpu.VMEM((2, nb, nb), BF16),
            pltpu.VMEM((2, rows, nb), BF16),
            dma((8,)),
            pltpu.VMEM((2, rows, nb), BF16),
            pltpu.VMEM((CORES, 2, rows, nb), BF16),
            pltpu.VMEM((nb, CORES * 2 * rows), BF16),
            pltpu.VMEM((CORES, 2, rows, nb), BF16),
            pltpu.VMEM((2, nb, nb), BF16),
            pltpu.VMEM((nb, nb), F32),
            pltpu.VMEM((A_CHUNKS, a_rows, nb), F32),
            pltpu.VMEM((A_CHUNKS, a_rows, nb), BF16),
            pltpu.VMEM((2, A_CHUNKS, a_rows, nb), BF16),
            pltpu.VMEM((A_CHUNKS, a_rows, nb), BF16),
            pltpu.VMEM((A_CHUNKS, a_rows, nb), BF16),
            pltpu.VMEM((strips, 2, nb, LANES), F32),
            pltpu.VMEM((strips, 2, nb, LANES), BF16),
            pltpu.VMEM((2, strips, 2, nb, LANES), BF16),
            pltpu.VMEM((strips, 2, nb, LANES), BF16),
            pltpu.VMEM((CORES, A_CHUNKS, a_rows, nb), BF16),
            pltpu.VMEM((nb, 2 * nb), BF16),
            pltpu.VMEM((nb, 2 * nb), F32),
            pltpu.VMEM((2, nb, nb), BF16),
            dma((5,)),
            dma((5,)),
            dma((2,)),
            dma((3,)),
            dma((CORES, strips)),
            dma((CORES, U_PIECES)),
            dma((1,)),
            dma((CORES, A_CHUNKS)),
            dma((1,)),
            dma((2, A_CHUNKS)),
            dma((1,)),
            dma((1,)),
            dma((2, c_total)),
            dma((1,)),
        ],
        compiler_params=pltpu.CompilerParams(
            collective_id=0, has_side_effects=True, vmem_limit_bytes=56 << 20
        ),
    )(band_coeffs[0], cutoff_weight, row_order, gauge_matrix[0])
    correlations, whitened = pl.pallas_call(
        functools.partial(finish, ka_count),
        out_shape=(
            jax.ShapeDtypeStruct((2, 2, nb, nb), F32),
            jax.ShapeDtypeStruct((2, rows, nb), BF16),
        ),
        in_specs=[hbm, hbm, hbm],
        out_specs=(hbm, hbm),
        scratch_shapes=[
            pltpu.VMEM((2, 2, nb, nb), BF16),
            pltpu.VMEM((2, rows, nb), BF16),
            pltpu.SMEM((1,), jnp.int32),
            pltpu.VMEM((2, 2, nb, nb), F32),
            dma((6,)),
            dma((5,)),
        ],
        compiler_params=pltpu.CompilerParams(vmem_limit_bytes=56 << 20),
    )(pair, whitened, neighbour)
    return (whitened[None], correlations[None])


def solution(mesh):
    in_specs = (
        P("ka", None, "pw", None),
        P("ka", "pw"),
        P("ka", "pw"),
        P("ka"),
        P("ka", None, None, None),
    )
    out_specs = (P("ka", None, "pw", None), P("ka", None, None, None, None))
    return jax.shard_map(
        functools.partial(on_device, mesh.shape["ka"], mesh.shape["pw"]),
        mesh=mesh, in_specs=in_specs, out_specs=out_specs, check_vma=False,
    )
```

```python
import functools
import math

import jax
import jax.numpy as jnp
from jax import lax
from jax.experimental import pallas as pl
from jax.experimental.pallas import tpu as pltpu
from jax.sharding import PartitionSpec as P

MESH = pl.DeviceIdType.MESH
CORES = 2
LANES = 128
A_CHUNKS = 4
U_PIECES = 2
PARTS = 4
NEAR_STEPS = ((4, 8, 0, 3), (8, 12, 3, 8), (12, 12, 8, 12), (12, 12, 12, 12), (12, 12, 12, 12), (12, 12, 12, 12), (12, 12, 12, 12))
FAR_STEPS = ((0,0,0,0),(0,0,0,0),(0,1,0,0),(1,3,0,0),(3,9,0,3),(9,12,3,6),(12,12,6,12))
F32 = jnp.float32
BF16 = jnp.bfloat16


def mm(left, right):
    return jnp.dot(left, right, preferred_element_type=F32)


def mm_t(left, right):
    return lax.dot_general(left, right, (((0,), (0,)), ((), ())), preferred_element_type=F32)


def complex_mm(left_re, left_im, right_re, right_im):
    width = right_re.shape[1]
    left = jnp.concatenate([left_re, left_im], axis=1)
    right = jnp.concatenate(
        [
            jnp.concatenate([right_re, right_im], axis=1),
            jnp.concatenate([-right_im, right_re], axis=1),
        ],
        axis=0,
    )
    both = mm(left, right)
    return both[:, :width], both[:, width:]


def halves(packed):
    turned = packed.T
    return 0.5 * (packed + turned), 0.5 * (packed - turned)


def kernel(
    ka_count,
    pw_count,
    bands_hbm,
    weight_hbm,
    order_hbm,
    gauge_hbm,
    white_out,
    corr_out,
    bands_ref,
    weight_ref,
    order_ref,
    gauge_ref,
    white_buf,
    load_sem,
    f_buf,
    p_buf,
    own_t,
    fn_buf,
    un_buf,
    a_full,
    a_local,
    a_sum,
    a_in,
    a_tot,
    a_other,
    c_local,
    c_sum,
    c_in,
    c_tot,
    an_buf,
    v_buf,
    x_buf,
    r_buf,
    pair_send,
    pair_recv,
    x_send,
    y_send,
    fn_recv,
    un_recv,
    an_send,
    an_recv,
    a_send,
    a_recv,
    a_out,
    c_send,
    c_recv,
    c_out,
):
    rows, nb = bands_ref.shape[1], bands_ref.shape[2]
    loads = [
        pltpu.make_async_copy(src, dst, load_sem.at[turn])
        for turn, (src, dst) in enumerate(
            [
                (bands_hbm, bands_ref),
                (weight_hbm, weight_ref),
                (order_hbm, order_ref),
                (gauge_hbm, gauge_ref),
            ]
        )
    ]
    for load in loads:
        load.start()
    half = nb // CORES
    strips = nb // LANES
    a_rows = half // A_CHUNKS
    u_rows = nb // U_PIECES
    c_total = PARTS * strips
    k = lax.axis_index("ka")
    p = lax.axis_index("pw")
    core = lax.rem(p, CORES)
    q = lax.div(p, CORES)
    line = pw_count // CORES
    base = q * CORES
    partner = base + 1 - core
    parity = lax.rem(k, 2)
    near = core == parity
    far = core != parity
    across = k + 1 - 2 * parity
    across_core = base + 1 - parity
    onward = lax.rem(k + 2 - 4 * parity + ka_count, ka_count)
    source = lax.rem(k - 2 + 4 * parity + ka_count, ka_count)
    edge = (q == 0) | (q == line - 1)
    inner = jnp.logical_not(edge)
    mid = (q == line // 2 - 1) | (q == line // 2)
    slot = mid.astype(jnp.int32)
    side_sign = jnp.where(2 * q < line, 1, -1)
    inward = p + CORES * side_sign
    outward = p - CORES * side_sign

    barrier = pltpu.get_barrier_semaphore()

    def greet(a, b):
        pl.semaphore_signal(barrier, inc=1, device_id=(a, b), device_id_type=MESH)

    greet(k, partner)
    greet(k, inward)

    @pl.when(near)
    def _():
        for side in range(CORES):
            greet(across, base + side)

    @pl.when(far)
    def _():
        greet(source, partner)

    @pl.when(inner)
    def _():
        greet(k, outward)

    eye = (
        lax.broadcasted_iota(jnp.int32, (nb, nb), 0) == lax.broadcasted_iota(jnp.int32, (nb, nb), 1)
    ).astype(F32)
    first = lax.broadcasted_iota(jnp.int32, (nb, nb), 0) == 0
    rest = jnp.where(first, 0.0, eye)

    for load in loads[:3]:
        load.wait()
    row_id = lax.broadcasted_iota(jnp.int32, (rows, rows), 0)
    col_id = lax.broadcasted_iota(jnp.int32, (rows, rows), 1)
    weight = jnp.sum(jnp.where(row_id == col_id, weight_ref[...], 0.0), axis=1, keepdims=True)
    pick = (row_id == order_ref[...] - p * rows).astype(BF16)
    for part in range(2):
        filtered = (bands_ref[part].astype(F32) * weight).astype(BF16)
        f_buf[part] = filtered
        p_buf[core, part] = mm(pick, filtered).astype(BF16)

    as_one = lambda flag: flag.astype(jnp.int32)
    pl.semaphore_wait(barrier, 3 + as_one(near) + as_one(inner))

    def remote(src, dst, send, recv, a, b):
        return pltpu.make_async_remote_copy(
            src_ref=src, dst_ref=dst, send_sem=send, recv_sem=recv,
            device_id=(a, b), device_id_type=MESH,
        )

    def to_pair(src, dst, turn):
        return remote(src, dst, pair_send.at[turn], pair_recv.at[turn], k, partner)

    def got_pair(dst, turn):
        remote(dst, dst, pair_send.at[turn], pair_recv.at[turn], k, partner).wait_recv()

    def to_across(src, dst, recv, turn):
        return remote(src, dst, x_send.at[turn], recv, across, across_core)

    def arrived(dst, recv):
        remote(dst, dst, x_send.at[0], recv, k, partner).wait_recv()

    def pass_on(dst, recv, turn):
        return remote(dst, dst, y_send.at[turn], recv, onward, partner)

    def strip_of(buf, t):
        return buf.at[:, :, pl.ds(t * LANES, LANES)]

    p_copy = to_pair(p_buf.at[core], p_buf.at[core], 0)
    p_copy.start()
    x_copies = [
        to_across(strip_of(f_buf, t), strip_of(fn_buf.at[core], t), fn_recv.at[core, t], 0)
        for t in range(strips)
    ]
    for copy in x_copies:
        copy.start()
    for load in loads[3:]:
        load.wait()
    u_parts = [(side, piece) for piece in range(U_PIECES) for side in range(CORES)]

    def u_piece(side, piece):
        return un_buf.at[side, pl.ds(piece * u_rows, u_rows)]

    for piece in range(U_PIECES):
        u_copy = to_across(
            gauge_ref.at[core, pl.ds(piece * u_rows, u_rows)], u_piece(core, piece),
            un_recv.at[core, piece], 1,
        )
        u_copy.start()

    f_passed = [
        [
            pass_on(strip_of(fn_buf.at[side], t), fn_recv.at[side, t], 0)
            for side in range(CORES)
        ]
        for t in range(strips)
    ]
    u_passed = [
        pass_on(u_piece(side, piece), un_recv.at[side, piece], 1)
        for side, piece in u_parts
    ]
    n_parts = [(side, i) for i in range(A_CHUNKS) for side in range(CORES)]
    n_passed = [
        pass_on(an_buf.at[side, i], an_recv.at[side, i], 2)
        for side, i in n_parts
    ]

    def pass_a():
        for n, (side, i) in enumerate(n_parts):
            arrived(an_buf.at[side, i], an_recv.at[side, i])
            n_passed[n].start()

    got_pair(p_buf.at[1 - core], 0)
    own_flat = p_buf[...].reshape(CORES * 2 * rows, nb)
    turned = []
    for side in range(CORES):
        turned += [p_buf[side, 1], -p_buf[side, 0]]
    own_turned = jnp.concatenate(turned, axis=0)
    own_t[...] = own_flat.T
    gram = mm(own_t[...], own_flat) + mm(own_t[...], own_turned)
    a_full[...] = gram - (jnp.sum(gram * eye) / nb) * rest
    for i in range(A_CHUNKS):
        a_local[i] = a_full[pl.ds(pl.multiple_of(core * half + i * a_rows, 8), a_rows), :]

    def c_view(buf, i):
        t = lax.div(i, PARTS)
        part = lax.div(lax.rem(i, PARTS), 2)
        low = pl.multiple_of(lax.rem(i, 2) * half, 16)
        return buf.at[t, part, pl.ds(low, half)]

    def a_view(buf, i):
        return buf.at[i]

    def gather(view, local, total, incoming, send, recv, i):
        @pl.when(edge)
        def _():
            view(total, i)[...] = view(local, i)[...].astype(BF16)

        @pl.when(inner)
        def _():
            arrived(view(incoming.at[0], i), recv.at[0, i])
            view(total, i)[...] = (
                view(local, i)[...] + view(incoming.at[0], i)[...].astype(F32)
            ).astype(BF16)

        remote(
            view(total, i), view(incoming.at[slot], i), send.at[0], recv.at[slot, i], k, inward
        ).start()

    def spread(view, total, incoming, final, recv, out, i):
        @pl.when(mid)
        def _():
            arrived(view(incoming.at[1], i), recv.at[1, i])
            view(final, i)[...] = (
                view(total, i)[...].astype(F32) + view(incoming.at[1], i)[...].astype(F32)
            ).astype(BF16)

        @pl.when(jnp.logical_not(mid))
        def _():
            arrived(view(final, i), recv.at[1, i])

        @pl.when(inner)
        def _():
            remote(view(final, i), view(final, i), out.at[0], recv.at[1, i], k, outward).start()

    def gather_a(i):
        gather(a_view, a_local, a_sum, a_in, a_send, a_recv, i)

    def share_a(i):
        return remote(
            a_tot.at[i], an_buf.at[core, i], an_send.at[0], an_recv.at[core, i], across, across_core
        )

    def spread_a(i):
        spread(a_view, a_sum, a_in, a_tot, a_recv, a_out, i)
        share_a(i).start()

    def gather_c(i):
        gather(c_view, c_local, c_sum, c_in, c_send, c_recv, i)

    def spread_c(i):
        spread(c_view, c_sum, c_in, c_tot, c_recv, c_out, i)

    def over(one, start, stop):
        def step(i, carry):
            one(i)
            return carry

        lax.fori_loop(start, stop, step, 0)

    def at_cut(cut):
        return cut * c_total // 12

    def sums(turn):
        bounds = [
            jnp.where(near, at_cut(a), at_cut(b)) for a, b in zip(NEAR_STEPS[turn], FAR_STEPS[turn])
        ]
        g_low, g_high, s_low, s_high = bounds

        @pl.when(inner)
        def _():
            def one(n):
                @pl.when(g_low + n < g_high)
                def _():
                    gather_c(g_low + n)

                @pl.when(s_low + n < s_high)
                def _():
                    spread_c(s_low + n)

            over(one, 0, jnp.maximum(g_high - g_low, s_high - s_low))

    a_copy = to_pair(a_tot, a_other, 1)

    def get_strip(t, forward):
        for side in range(CORES):
            arrived(strip_of(fn_buf.at[side], t), fn_recv.at[side, t])
            if forward:
                f_passed[t][side].start()

    def cross_strip(t):
        low, high = t * LANES, (t + 1) * LANES
        plain, other = [], []
        for side in range(CORES):
            re, im = fn_buf[side, 0, :, low:high], fn_buf[side, 1, :, low:high]
            plain += [re, im]
            other += [im, -re]
        right = jnp.concatenate(
            [jnp.concatenate(plain, axis=0), jnp.concatenate(other, axis=0)], axis=1
        )
        cross = mm(own_t[...], right)
        c_local[t, 0] = cross[:, :LANES]
        c_local[t, 1] = cross[:, LANES:]

    def edge_strip(t):
        @pl.when(edge)
        def _():
            over(gather_c, PARTS * t, PARTS * (t + 1))

    def pass_u(piece):
        for n, (side, own) in enumerate(u_parts):
            if own == piece:
                arrived(u_piece(side, piece), un_recv.at[side, piece])
                u_passed[n].start()

    @pl.when(edge)
    def _():
        over(gather_a, 0, A_CHUNKS)

    a_cuts = [A_CHUNKS * t // strips for t in range(strips + 1)]

    @pl.when(near)
    def _():
        for t in range(strips):
            get_strip(t, True)

            @pl.when(inner)
            def _():
                over(gather_a, a_cuts[t], a_cuts[t + 1])

            cross_strip(t)
            edge_strip(t)

        @pl.when(inner)
        def _():
            over(gather_c, 0, at_cut(2))
            over(spread_a, 0, A_CHUNKS // 2)
            over(gather_c, at_cut(2), at_cut(4))
            over(spread_a, A_CHUNKS // 2, A_CHUNKS)
            a_copy.start()
            pass_u(0)
            sums(0)

    @pl.when(far)
    def _():
        @pl.when(inner)
        def _():
            over(gather_a, 0, A_CHUNKS)
            over(spread_a, 0, A_CHUNKS)
            a_copy.start()

        for t in range(strips):
            get_strip(t, False)
            cross_strip(t)
            edge_strip(t)

    @pl.when(edge)
    def _():
        @pl.when(near)
        def _():
            for piece in range(U_PIECES):
                pass_u(piece)

        over(spread_a, 0, A_CHUNKS)
        a_copy.start()
        pl.when(near)(pass_a)

    @pl.when(near & inner)
    def _():
        for piece in range(1, U_PIECES):
            pass_u(piece)

    sums(1)
    pl.when(near & inner)(pass_a)
    sums(2)
    got_pair(a_other, 1)
    a_full[pl.ds(pl.multiple_of(core * half, 8), half), :] = (
        a_tot[...].astype(F32).reshape(half, nb)
    )
    a_full[pl.ds(pl.multiple_of((1 - core) * half, 8), half), :] = (
        a_other[...].astype(F32).reshape(half, nb)
    )

    def newton(packed, between):
        mean = jnp.sum(packed * eye)
        deviation = packed - mean * (eye - rest)
        e_re, e_im = halves(deviation * (0.5 / mean))
        e_re_b, e_im_b = e_re.astype(BF16), e_im.astype(BF16)
        sq_re, sq_im = complex_mm(e_re_b, e_im_b, e_re_b, e_im_b)
        between()
        left_re, left_im = e_re - 0.5 * sq_re, e_im - 0.5 * sq_im
        right_re, right_im = 0.25 * sq_re - 1.25 * e_re, 0.25 * sq_im - 1.25 * e_im
        last_re, last_im = complex_mm(
            left_re.astype(BF16), left_im.astype(BF16), right_re.astype(BF16), right_im.astype(BF16)
        )
        white_re = (
            1.38671875 * eye - 0.75 * e_re - 0.78125 * left_re - 0.3125 * right_re - 0.5 * last_re
        )
        white_im = -0.75 * e_im - 0.78125 * left_im - 0.3125 * right_im - 0.5 * last_im
        return white_re.astype(BF16), white_im.astype(BF16)

    w_re, w_im = newton(a_full[...], lambda: sums(3))
    sums(4)
    out_re, out_im = complex_mm(f_buf[0], f_buf[1], w_re, w_im)
    white_buf[0] = out_re.astype(BF16)
    white_buf[1] = out_im.astype(BF16)
    stores = [pltpu.make_async_copy(white_buf, white_out, load_sem.at[4])]
    stores[0].start()
    sums(5)
    root = math.sqrt(rows * pw_count)
    v_re = mm_t(gauge_ref[0], w_re) + mm_t(gauge_ref[1], w_im)
    v_im = mm_t(gauge_ref[0], w_im) - mm_t(gauge_ref[1], w_re)
    v_buf[:, :nb] = (v_re * root).astype(BF16)
    v_buf[:, nb:] = (v_im * root).astype(BF16)
    sums(6)

    @pl.when(far)
    def _():
        for side, piece in u_parts:
            arrived(u_piece(side, piece), un_recv.at[side, piece])
        for side, i in n_parts:
            arrived(an_buf.at[side, i], an_recv.at[side, i])

    next_re, next_im = newton(an_buf[...].astype(F32).reshape(nb, nb), lambda: None)
    vn_re, vn_im = complex_mm(next_re, next_im, un_buf[0], un_buf[1])
    vn_re, vn_im = vn_re.astype(BF16), vn_im.astype(BF16)
    moved = None
    for low, high in ((0, strips - 1), (strips - 1, strips)):
        @pl.when(edge)
        def _():
            over(spread_c, PARTS * low, PARTS * high)

        left = jnp.concatenate(
            [c_tot[t, part] for part in range(2) for t in range(low, high)], axis=1
        )
        re, im = vn_re[low * LANES : high * LANES], vn_im[low * LANES : high * LANES]
        right = jnp.concatenate(
            [jnp.concatenate([re, im], axis=1), jnp.concatenate([-im, re], axis=1)], axis=0
        )
        if low == 0:
            x_buf[...] = mm(left, right)
        else:
            moved = x_buf[...] + mm(left, right)
    x_re, x_im = moved[:, :nb].astype(BF16), moved[:, nb:].astype(BF16)
    right = jnp.concatenate(
        [jnp.concatenate([x_re, x_im], axis=1), jnp.concatenate([-x_im, x_re], axis=1)], axis=0
    )
    blocks = [(0, 0, nb), (1, 0, nb - 2 * LANES), (1, nb - 2 * LANES, nb)]
    r_copies = []
    for n, (part, low, high) in enumerate(blocks):
        cols = pl.ds(low, high - low)
        own, there = r_buf.at[part, :, cols], corr_out.at[core, part, :, cols]
        r_copies.append(to_pair(own, there, 2 + n))
        stores.append(pltpu.make_async_copy(own, there, load_sem.at[5 + n]))
    edge_col = 2 * nb - 2 * LANES
    result = mm(v_buf[...], right[:, :edge_col])
    r_buf[0] = result[:, :nb].astype(BF16)
    r_copies[0].start()
    stores[1].start()
    r_buf[1, :, : nb - 2 * LANES] = result[:, nb:].astype(BF16)
    r_copies[1].start()
    stores[2].start()
    r_buf[1, :, nb - 2 * LANES :] = mm(v_buf[...], right[:, edge_col:]).astype(BF16)
    r_copies[2].start()
    stores[3].start()

    def all_sent(buf, send):
        remote(buf, buf, send, pair_recv.at[0], k, partner).wait_send()

    for copy in [p_copy, a_copy]:
        copy.wait_send()
    all_sent(f_buf, x_send.at[0])
    all_sent(gauge_ref.at[core], x_send.at[1])
    all_sent(a_tot, an_send.at[0])
    all_sent(a_sum, a_send.at[0])
    all_sent(c_sum, c_send.at[0])

    @pl.when(near)
    def _():
        for turn, buf in enumerate((fn_buf, un_buf, an_buf)):
            all_sent(buf, y_send.at[turn])

    @pl.when(inner)
    def _():
        all_sent(a_tot, a_out.at[0])
        all_sent(c_tot, c_out.at[0])

    for n, (part, low, high) in enumerate(blocks):
        got_pair(corr_out.at[1 - core, part, :, pl.ds(low, high - low)], 2 + n)
    for store in stores:
        store.wait()
    for copy in r_copies:
        copy.wait_send()


def finish(
    ka_count, pair_hbm, white_hbm, neighbour_hbm, corr_hbm, whitened_hbm,
    pair_ref, white_ref, neighbour_ref, corr_ref, load_sem, store_sem,
):
    parts = [(d, part) for d in range(2) for part in range(2)]
    order = pltpu.make_async_copy(neighbour_hbm, neighbour_ref, load_sem.at[5])
    order.start()
    loads = [
        pltpu.make_async_copy(pair_hbm.at[d, part], pair_ref.at[d, part], load_sem.at[n])
        for n, (d, part) in enumerate(parts)
    ] + [pltpu.make_async_copy(white_hbm, white_ref, load_sem.at[4])]
    for load in loads:
        load.start()
    order.wait()
    looks_ahead = neighbour_ref[0] == lax.rem(lax.axis_index("ka") + 1, ka_count)
    flip = 1 - looks_ahead.astype(jnp.int32)
    stores = [
        pltpu.make_async_copy(
            corr_ref.at[d, part], corr_hbm.at[d + flip - 2 * d * flip, part], store_sem.at[n]
        )
        for n, (d, part) in enumerate(parts)
    ] + [pltpu.make_async_copy(white_ref, whitened_hbm, store_sem.at[4])]
    for n, (d, part) in enumerate(parts):
        loads[n].wait()
        corr_ref[d, part] = pair_ref[d, part].astype(F32)
        stores[n].start()
    loads[4].wait()
    stores[4].start()
    for store in stores:
        store.wait()


def on_device(ka_count, pw_count, band_coeffs, cutoff_weight, row_order, neighbour, gauge_matrix):
    rows, nb = band_coeffs.shape[2], band_coeffs.shape[3]
    half = nb // CORES
    strips = nb // LANES
    a_rows = half // A_CHUNKS
    c_total = PARTS * strips
    hbm = pl.BlockSpec(memory_space=pltpu.HBM)
    dma = pltpu.SemaphoreType.DMA
    whitened, pair = pl.pallas_call(
        functools.partial(kernel, ka_count, pw_count),
        out_shape=(
            jax.ShapeDtypeStruct((2, rows, nb), BF16),
            jax.ShapeDtypeStruct((2, 2, nb, nb), BF16),
        ),
        in_specs=[hbm] * 4,
        out_specs=(hbm, hbm),
        scratch_shapes=[
            pltpu.VMEM((2, rows, nb), BF16),
            pltpu.VMEM((1, rows), F32),
            pltpu.VMEM((1, rows), jnp.int32),
            pltpu.VMEM((2, nb, nb), BF16),
            pltpu.VMEM((2, rows, nb), BF16),
            dma((8,)),
            pltpu.VMEM((2, rows, nb), BF16),
            pltpu.VMEM((CORES, 2, rows, nb), BF16),
            pltpu.VMEM((nb, CORES * 2 * rows), BF16),
            pltpu.VMEM((CORES, 2, rows, nb), BF16),
            pltpu.VMEM((2, nb, nb), BF16),
            pltpu.VMEM((nb, nb), F32),
            pltpu.VMEM((A_CHUNKS, a_rows, nb), F32),
            pltpu.VMEM((A_CHUNKS, a_rows, nb), BF16),
            pltpu.VMEM((2, A_CHUNKS, a_rows, nb), BF16),
            pltpu.VMEM((A_CHUNKS, a_rows, nb), BF16),
            pltpu.VMEM((A_CHUNKS, a_rows, nb), BF16),
            pltpu.VMEM((strips, 2, nb, LANES), F32),
            pltpu.VMEM((strips, 2, nb, LANES), BF16),
            pltpu.VMEM((2, strips, 2, nb, LANES), BF16),
            pltpu.VMEM((strips, 2, nb, LANES), BF16),
            pltpu.VMEM((CORES, A_CHUNKS, a_rows, nb), BF16),
            pltpu.VMEM((nb, 2 * nb), BF16),
            pltpu.VMEM((nb, 2 * nb), F32),
            pltpu.VMEM((2, nb, nb), BF16),
            dma((5,)),
            dma((5,)),
            dma((2,)),
            dma((3,)),
            dma((CORES, strips)),
            dma((CORES, U_PIECES)),
            dma((1,)),
            dma((CORES, A_CHUNKS)),
            dma((1,)),
            dma((2, A_CHUNKS)),
            dma((1,)),
            dma((1,)),
            dma((2, c_total)),
            dma((1,)),
        ],
        compiler_params=pltpu.CompilerParams(
            collective_id=0, has_side_effects=True, vmem_limit_bytes=56 << 20
        ),
    )(band_coeffs[0], cutoff_weight, row_order, gauge_matrix[0])
    correlations, whitened = pl.pallas_call(
        functools.partial(finish, ka_count),
        out_shape=(
            jax.ShapeDtypeStruct((2, 2, nb, nb), F32),
            jax.ShapeDtypeStruct((2, rows, nb), BF16),
        ),
        in_specs=[hbm, hbm, hbm],
        out_specs=(hbm, hbm),
        scratch_shapes=[
            pltpu.VMEM((2, 2, nb, nb), BF16),
            pltpu.VMEM((2, rows, nb), BF16),
            pltpu.SMEM((1,), jnp.int32),
            pltpu.VMEM((2, 2, nb, nb), F32),
            dma((6,)),
            dma((5,)),
        ],
        compiler_params=pltpu.CompilerParams(vmem_limit_bytes=56 << 20),
    )(pair, whitened, neighbour)
    return (whitened[None], correlations[None])


def solution(mesh):
    in_specs = (
        P("ka", None, "pw", None),
        P("ka", "pw"),
        P("ka", "pw"),
        P("ka"),
        P("ka", None, None, None),
    )
    out_specs = (P("ka", None, "pw", None), P("ka", None, None, None, None))
    return jax.shard_map(
        functools.partial(on_device, mesh.shape["ka"], mesh.shape["pw"]),
        mesh=mesh, in_specs=in_specs, out_specs=out_specs, check_vma=False,
    )
```
